32 devices in a mesh: grp: 2 (over y), seq: 4 (over z), mask: 2 (over x), head: 2 (over core).
Axes of the slice: x: 2, y: 2, z: 4, core: 2. Of those that a mesh axis runs over, the one named last changes fastest.
Arguments:
- dna: bfloat16 [1024, 512], P(('grp', 'seq')), parts along dimension 0, may hold values from 0 to 1, as said below
- offsets: int32 [4], P('grp'), parts along dimension 0, may hold values from 0 to 63488
- stem_weight: bfloat16 [512, 1536], P(None, ('mask', 'head')), may hold values from -0.5 to 0.5
- conv_weight: bfloat16 [5, 1536, 1536], P(None, None, ('mask', 'head')), may hold values from -0.0625 to 0.0625
- qkv_weight: bfloat16 [1536, 3, 4, 192], P(None, None, 'head', 'mask'), may hold values from -0.17860863 to 0.17860863
- out_weight: bfloat16 [768, 1536], P('head'), may hold values from -0.5 to 0.5
Outputs:
- mixed: bfloat16 [4, 512, 1536], P(('grp', 'mask'), 'seq', 'head'), parts along dimension 0
The draws below stay inside these ranges and needn't reach their ends.
There are 2 independent parts, one for each index of `grp`. The reference program is written for one: setup_inputs(seed, part) draws one part's arguments, and reference() takes and returns one part's arrays. A program takes and returns all parts, laid end to end along the dimension named above; an argument that names none is the same for every part. Nothing has to cross between parts.
Inputs may be any that keep to these rules, and one draw needn't show every extreme that they name: `dna`: each token row is one-hot over the four channels of every base pair. `offsets`: each window lies inside the sequence of 65536 base pairs.
All inputs are finite; a program needn't handle non-finite values.
Results may differ from the reference program's by a relative error of at most 0.01.
Values may be sent and summed in bfloat16 or wider, within the bound.
A program may use at most 64 MiB of HBM per device.

```python
import math
import jax
import jax.numpy as jnp
from jax import lax

D = 1536
HEADS = 4
HD = 192
BPT = 128
KW = 5
TOKEN_FEATURES = 512
WIN_BP = 2048
WROWS = 24
TOKENS = 512
MASKS = 2


def draw_dna(key, part):
    bases = jax.random.randint(key, (TOKENS, BPT), 0, 4)
    return jax.nn.one_hot(bases, 4, dtype=jnp.float32).reshape(TOKENS, BPT * 4).astype(jnp.bfloat16)


def draw_qkv_weight(key, part):
    first_key = jax.random.fold_in(jax.random.fold_in(key, 17), 0)
    shape_all = (D, 3, HEADS, HD)
    spread = jnp.array([2.0, 2.0, 1.0], jnp.float32)[None, :, None, None] ** 0.5
    raw = jnp.clip(jax.random.normal(first_key, shape_all, jnp.float32), -4.0, 4.0)
    weight = raw * spread / math.sqrt(D)
    return jnp.clip(weight, -7.0 / math.sqrt(D), 7.0 / math.sqrt(D)).astype(jnp.bfloat16)


def block_levels(key, shape, pieces, smallest, top_value):
    level, own = 1.0, jax.random.fold_in(key, 6)
    for position, blocks in pieces:
        heights = jnp.exp(jax.random.uniform(jax.random.fold_in(own, position), (blocks,), jnp.float32, smallest / len(pieces), top_value / len(pieces)))
        level = level * jnp.repeat(heights, shape[position] // blocks).reshape([-1 if axis == position else 1 for axis in range(len(shape))])
    return level


def gaussian(key, extent, width, reach, pieces=(), kind=jnp.bfloat16):
    values = jax.random.normal(key, extent, jnp.float32) * width
    if len(pieces) > 0:
        values = block_levels(key, extent, pieces, -0.22, 0.18) * values
    return jnp.clip(values, min=-reach, max=reach).astype(kind)


def setup_inputs(seed: int = 0, part: int = 0) -> dict:
    key_of = jax.random.split(jax.random.key(seed), 7)
    own_keys = jax.random.split(jax.random.fold_in(key_of[6], part), 7)
    dna = draw_dna(jax.random.fold_in(jax.random.fold_in(key_of[6], part), 71), part)
    offsets = jax.random.randint(own_keys[1], (MASKS,), 0, TOKENS * BPT - WIN_BP + 1).astype(jnp.int32)
    stem_weight = gaussian(key_of[2], (TOKEN_FEATURES, D), BPT ** -0.5, 0.5, ((1, 4),))
    conv_weight = gaussian(key_of[3], (KW, D, D), (KW * D) ** -0.5, 0.0625, ((2, 4),))
    qkv_weight = draw_qkv_weight(jax.random.fold_in(key_of[6], 71), part)
    out_weight = gaussian(key_of[5], (HEADS * HD, D), (HEADS * HD // 5) ** -0.5, 0.5, ((0, 2),))
    return {"dna": dna, "offsets": offsets, "stem_weight": stem_weight, "conv_weight": conv_weight, "qkv_weight": qkv_weight, "out_weight": out_weight}


def conv_all(embedded, conv_weight, out_rows):
    summed = jnp.zeros((out_rows, conv_weight.shape[2]), jnp.float32)
    for kernel_tap in range(KW):
        summed = summed + jnp.dot(embedded[kernel_tap:kernel_tap + out_rows], conv_weight[kernel_tap], preferred_element_type=jnp.float32)
    return summed

def project_rows(trunk_rows, qkv_flat):
    wide = trunk_rows.astype(jnp.float32)
    normed = (wide * lax.rsqrt(lax.optimization_barrier(jnp.mean(wide * wide, axis=1, keepdims=True)) + 1e-06)).astype(jnp.bfloat16)
    projected = jnp.dot(normed, qkv_flat, preferred_element_type=jnp.float32).astype(jnp.bfloat16)
    return projected.reshape(trunk_rows.shape[0], 3, HEADS, HD)

def reference(dna, offsets, stem_weight, conv_weight, qkv_weight, out_weight):
    margin = KW // 2
    padded_dna = jnp.pad(dna, ((margin, margin), (0, 0)))
    embedded = jnp.dot(padded_dna, stem_weight, preferred_element_type=jnp.float32).astype(jnp.bfloat16)
    trunk = (embedded[margin:margin + TOKENS].astype(jnp.float32) + jax.nn.gelu(conv_all(embedded, conv_weight, TOKENS))).astype(jnp.bfloat16)
    qkv_flat = qkv_weight.reshape(D, 3 * HEADS * HD)
    base_rows = project_rows(trunk, qkv_flat)
    span_rows = WROWS + 2 * margin
    row_steps = lax.iota(jnp.int32, span_rows)
    base_pair = lax.iota(jnp.int32, TOKEN_FEATURES) // 4

    def one_mask(offset):
        first_token = (offset // BPT).astype(jnp.int32)
        window_start = jnp.clip(first_token - margin, 0, TOKENS - WROWS).astype(jnp.int32)
        window_dna = lax.dynamic_slice_in_dim(padded_dna, window_start, span_rows, 0)
        positions = (window_start - margin + row_steps)[:, None] * BPT + base_pair[None, :]
        inside = (positions >= offset) & (positions < offset + WIN_BP)
        masked = jnp.where(inside, jnp.zeros_like(window_dna), window_dna)
        window_emb = jnp.dot(masked, stem_weight, preferred_element_type=jnp.float32).astype(jnp.bfloat16)
        window_trunk = (window_emb[margin:margin + WROWS].astype(jnp.float32) + jax.nn.gelu(conv_all(window_emb, conv_weight, WROWS))).astype(jnp.bfloat16)
        merged = lax.dynamic_update_slice_in_dim(base_rows, project_rows(window_trunk, qkv_flat), window_start, 0)
        queries = merged[:, 0].astype(jnp.float32)
        key_rows = merged[:, 1].astype(jnp.float32)
        values = merged[:, 2].astype(jnp.float32)
        scores = jnp.einsum('qhc,khc->hqk', queries, key_rows) * HD ** (-0.5)
        raised = jnp.exp(scores - lax.optimization_barrier(jnp.max(scores, axis=2, keepdims=True)))
        denominator = lax.optimization_barrier(jnp.sum(raised, axis=2))
        weighted = jnp.einsum('hqk,khc->hqc', raised.astype(jnp.bfloat16).astype(jnp.float32), values)
        attended = (weighted / denominator[:, :, None]).astype(jnp.bfloat16)
        attended = jnp.transpose(attended, (1, 0, 2)).reshape(TOKENS, HEADS * HD)
        return jnp.dot(attended, out_weight, preferred_element_type=jnp.float32).astype(jnp.bfloat16)
    return lax.map(one_mask, offsets)
```

```python
import jax
import jax.numpy as jnp
from jax import lax
from jax.experimental import pallas as pl
from jax.experimental.pallas import tpu as pltpu
from jax.sharding import PartitionSpec as P

BPT = 128
MASK_DEV = 1
WIN_BP = 2048
WROWS = 24


def padded(cells, sides, width):
    for axis, dim in sides:
        count = lax.axis_size(axis)
        ends = count - 1
        head = lax.slice_in_dim(cells, 0, width, axis=dim)
        tail = lax.slice_in_dim(cells, cells.shape[dim] - width, cells.shape[dim], axis=dim)
        cells = jnp.concatenate(
            [
                lax.ppermute(tail, axis, [(i, (i + 1) % count) for i in range(ends)]),
                cells,
                lax.ppermute(head, axis, [((i + 1) % count, i) for i in range(ends)]),
            ],
            axis=dim,
        )
    return cells


def conv_rows(source, weight, out_rows):
    summed = None
    for kernel_tap in range(weight.shape[0]):
        tap_rows = lax.slice_in_dim(source, kernel_tap, kernel_tap + out_rows, axis=source.ndim - 2)
        tap_term = jnp.einsum(
            "...rc,cd->...rd", tap_rows, weight[kernel_tap], preferred_element_type=jnp.float32
        )
        summed = tap_term if summed is None else summed + tap_term
    return summed


def local(dna, offsets, stem_weight, conv_weight, qkv_weight, out_weight):
    tok_rows, features = dna.shape
    margin = conv_weight.shape[0] // 2
    row_start = lax.axis_index("seq") * tok_rows
    masks_all = offsets.shape[0]
    window_rows = WROWS
    span_rows = window_rows + 2 * margin
    extended = padded(dna, (("seq", 0),), margin)
    first_token = offsets // BPT
    local_start = jnp.clip(first_token - margin - row_start, 0, tok_rows - window_rows)

    def cut_window(window_begin):
        return lax.dynamic_slice_in_dim(extended, window_begin, span_rows, 0)

    window_dna = jax.vmap(cut_window)(local_start)
    row_steps = lax.iota(jnp.int32, span_rows)
    base_pair = lax.iota(jnp.int32, features) // 4
    positions = (
        row_start + local_start[:, None, None] - margin + row_steps[None, :, None]
    ) * BPT + base_pair[None, None, :]
    inside = (positions >= offsets[:, None, None]) & (positions < offsets[:, None, None] + WIN_BP)
    masked = jnp.where(inside, jnp.zeros_like(window_dna), window_dna)
    stacked = jnp.concatenate([extended, masked.reshape(masks_all * span_rows, features)], 0)
    embedded = jnp.dot(stacked, stem_weight, preferred_element_type=jnp.float32).astype(
        jnp.bfloat16
    )
    columns = embedded.shape[1]
    base_length = tok_rows + 2 * margin
    shard_part = lax.all_gather(embedded, ("mask", "head"), axis=1, tiled=True)
    part_width = shard_part.shape[1]
    base_out = conv_rows(shard_part[:base_length], conv_weight, tok_rows)
    window_part = shard_part[base_length:].reshape(masks_all, span_rows, part_width)
    window_out = conv_rows(window_part, conv_weight, window_rows)
    convolved = jnp.concatenate([base_out, window_out.reshape(masks_all * window_rows, columns)], 0)
    window_emb = embedded[base_length:].reshape(masks_all, span_rows, columns)[
        :, margin : margin + window_rows
    ]
    own_embedded = jnp.concatenate(
        [
            embedded[margin : margin + tok_rows],
            window_emb.reshape(masks_all * window_rows, columns),
        ],
        0,
    )
    trunk_part = (own_embedded.astype(jnp.float32) + jax.nn.gelu(convolved)).astype(jnp.bfloat16)
    trunk = lax.all_gather(trunk_part, ("mask", "head"), axis=1, tiled=True)
    width_all = trunk.shape[1]
    first_own = lax.axis_index("mask") * MASK_DEV
    own_windows = lax.dynamic_slice_in_dim(
        trunk[tok_rows:].reshape(masks_all, window_rows, width_all), first_own, MASK_DEV, 0
    )
    trunk_rows = jnp.concatenate(
        [trunk[:tok_rows], own_windows.reshape(MASK_DEV * window_rows, width_all)], 0
    )
    wide = trunk_rows.astype(jnp.float32)
    normed = (wide * lax.rsqrt(jnp.mean(wide * wide, axis=1, keepdims=True) + 1e-06)).astype(
        jnp.bfloat16
    )
    projected = jnp.einsum(
        "rd,dthc->rthc",
        normed,
        lax.all_gather(qkv_weight, "mask", axis=3, tiled=True),
        preferred_element_type=jnp.float32,
    ).astype(jnp.bfloat16)
    heads_here = projected.shape[2]
    head_size = projected.shape[3]
    base_qkv = projected[:tok_rows]
    window_qkv = projected[tok_rows:].reshape(MASK_DEV, window_rows, 3, heads_here, head_size)
    own_start = lax.dynamic_slice_in_dim(local_start, first_own, MASK_DEV, 0)
    scaling = head_size ** (-0.5)
    merged = lax.dynamic_update_slice_in_dim(base_qkv, window_qkv[0], own_start[0], 0)
    queries = merged[:, 0]
    running_top = jnp.full((heads_here, tok_rows), -1e30, jnp.float32)
    key_part = lax.all_gather(merged[:, 1], "seq", axis=0, tiled=True)
    value_part = lax.all_gather(merged[:, 2], "seq", axis=0, tiled=True)
    scores = (
        jnp.einsum("qhc,khc->hqk", queries, key_part, preferred_element_type=jnp.float32) * scaling
    )
    new_top = jnp.maximum(running_top, jnp.max(scores, axis=2))
    raised = jnp.exp(scores - new_top[:, :, None])
    denominator = jnp.sum(raised, axis=2)
    weighted = jnp.einsum(
        "hqk,khc->hqc", raised.astype(jnp.bfloat16), value_part, preferred_element_type=jnp.float32
    )
    running_top, denominator, weighted = (new_top, denominator, weighted)
    results = [weighted / denominator[:, :, None]]
    attended = jnp.stack(results).astype(jnp.bfloat16)
    attended = jnp.transpose(attended, (0, 2, 1, 3)).reshape(
        MASK_DEV, tok_rows, heads_here * head_size
    )
    partial_sums = jnp.einsum(
        "mqc,cd->mqd", attended, out_weight, preferred_element_type=jnp.float32
    )
    mixed = lax.psum_scatter(
        partial_sums.astype(jnp.bfloat16), "head", scatter_dimension=2, tiled=True
    )
    return mixed


MESH = pl.DeviceIdType.MESH
HALO = 8
TILE = 16
EARLY = 80
GROUP = 8


def fused_kernel(
    offsets_ref, dna_ref, stem_hbm, conv_hbm, qkv_hbm, ow_hbm, out_ref,
    halo_lo, halo_hi, stem, cw, qw, ow, emb, emb_own, acc, trunk, kv, kv_x, qa, qs, q_x,
    part_x, part_in,
    w_sem, halo_send, halo_recv, ag_send, ag_recv, x_send, x_recv, z_send, z_recv, p_sem,
):
    rows, features = dna_ref.shape
    cols = stem.shape[1]
    piece = ow_hbm.shape[0] // 4
    wkv, nq = 4 * piece, 2 * piece
    shards = kv.shape[0]
    taps = cw.shape[1]
    margin = taps // 2
    spread = WIN_BP // BPT
    masks = offsets_ref.shape[0]
    m, h, s = lax.axis_index("mask"), lax.axis_index("head"), lax.axis_index("seq")
    row_start = s * rows
    core_peer = {"head": 1 - h}
    x_peer = {"mask": 1 - m}
    has_lo, has_hi = s > 0, s < shards - 1

    def remote(src, dst, send, recv, device):
        return pltpu.make_async_remote_copy(
            src_ref=src, dst_ref=dst, send_sem=send, recv_sem=recv,
            device_id=device, device_id_type=MESH,
        )

    barrier = pltpu.get_barrier_semaphore()
    for peer in (core_peer, x_peer):
        pl.semaphore_signal(barrier, inc=1, device_id=peer, device_id_type=MESH)

    @pl.when(has_lo)
    def _():
        pl.semaphore_signal(barrier, inc=1, device_id={"seq": s - 1}, device_id_type=MESH)

    @pl.when(has_hi)
    def _():
        pl.semaphore_signal(barrier, inc=1, device_id={"seq": s + 1}, device_id_type=MESH)

    slot_of = (2 * m + h, 2 * m + 1 - h, 2 * (1 - m) + h, 2 * (1 - m) + 1 - h)
    stem_copy = pltpu.make_async_copy(stem_hbm, stem, w_sem.at[0])
    stem_copy.start()
    conv_copies, qkv_copies, ow_copies = [], [], []
    for r in range(4):
        span = pl.ds(pl.multiple_of(slot_of[r] * cols, 128), cols)
        conv_copies.append(
            pltpu.make_async_copy(conv_hbm.at[:, span, :], cw.at[r], w_sem.at[1 + r])
        )
        conv_copies[r].start()
    for r in range(4):
        span = pl.ds(pl.multiple_of(slot_of[r] * cols, 128), cols)
        for k, (src, dst, count) in enumerate(((nq, 0, wkv), (0, wkv, nq))):
            copy = pltpu.make_async_copy(
                qkv_hbm.at[pl.ds(src, count), span],
                qw.at[r, pl.ds(dst, count), :],
                w_sem.at[13 + 2 * r + k],
            )
            copy.start()
            qkv_copies.append(copy)
    qw[:, wkv + nq :, :] = jnp.zeros((4, qw.shape[1] - wkv - nq, cols), qw.dtype)
    gap = ow.shape[1] - 2 * piece
    ow[:, 0:gap, :] = jnp.zeros((2, gap, ow.shape[2]), ow.dtype)
    for p, place in enumerate((m, 1 - m)):
        for hh in range(2):
            first = pl.multiple_of(hh * 2 * piece + place * piece, 16)
            copy = pltpu.make_async_copy(
                ow_hbm.at[pl.ds(first, piece), :],
                ow.at[p, pl.ds(gap + hh * piece, piece), :],
                w_sem.at[9 + 2 * p + hh],
            )
            copy.start()
            ow_copies.append(copy)
    past = HALO + rows + HALO
    stem_copy.wait()
    emb_inner = jnp.dot(
        dna_ref[...], stem[...], preferred_element_type=jnp.float32
    ).astype(jnp.bfloat16)
    emb[0, :rows] = emb_inner
    emb_own[HALO : HALO + rows] = emb_inner.astype(jnp.float32)

    pl.semaphore_wait(barrier, 2 + has_lo.astype(jnp.int32) + has_hi.astype(jnp.int32))

    to_hi = remote(
        dna_ref.at[pl.ds(rows - TILE, TILE), :], halo_lo, halo_send.at[0], halo_recv.at[0],
        {"seq": s + 1},
    )
    to_lo = remote(
        dna_ref.at[pl.ds(0, TILE), :], halo_hi, halo_send.at[1], halo_recv.at[1], {"seq": s - 1}
    )

    @pl.when(has_hi)
    def _():
        to_hi.start()

    @pl.when(has_lo)
    def _():
        to_lo.start()

    def gather(buf, g, cuts):
        def pair(src, dst, where, k, device):
            n = 3 * (2 * g + where) + k
            span = pl.ds(cuts[where], cuts[where + 1] - cuts[where])
            return remote(
                buf.at[src, span, :], buf.at[dst, span, :], ag_send.at[n], ag_recv.at[n], device
            )

        return [
            (pair(0, 1, w, 0, core_peer), pair(0, 2, w, 1, x_peer), pair(2, 3, w, 2, core_peer))
            for w in range(2)
        ]

    ready = EARLY + 2 * TILE
    (core_a, x_a, both_a), (core_b, x_b, both_b) = gather(emb, 0, (0, ready, rows + TILE))
    x_a.start()
    core_a.start()

    @pl.when(jnp.logical_not(has_lo))
    def _():
        halo_lo[...] = jnp.zeros(halo_lo.shape, halo_lo.dtype)

    @pl.when(jnp.logical_not(has_hi))
    def _():
        halo_hi[...] = jnp.zeros(halo_hi.shape, halo_hi.dtype)

    def conv(r, begin, end):
        for j in range(taps):
            term = jnp.dot(emb[r, begin:end], cw[r, j], preferred_element_type=jnp.float32)
            inner = min(end, rows) - begin
            if inner > 0:
                where = slice(HALO + begin, HALO + begin + inner)
                acc[j, where] = term[:inner] if r == 0 else acc[j, where] + term[:inner]
            if end > rows:
                low, high = term[inner : inner + HALO], term[inner + HALO :]
                acc[j, :HALO] = low if r == 0 else acc[j, :HALO] + low
                where = slice(HALO + rows, past)
                acc[j, where] = high if r == 0 else acc[j, where] + high

    conv_copies[0].wait()
    conv(0, 0, rows)

    @pl.when(has_lo)
    def _():
        to_hi.wait_recv()

    @pl.when(has_hi)
    def _():
        to_lo.wait_recv()

    def first_of(offset):
        return lax.shift_right_logical(offset, 7) - row_start

    edge = HALO + 2
    ext = jnp.concatenate([halo_lo[...], dna_ref[...], halo_hi[...]], 0)
    row = lax.broadcasted_iota(jnp.int32, (TILE, 1), 0)
    column = lax.shift_right_logical(lax.broadcasted_iota(jnp.int32, (TILE, features), 1), 2)
    source = jnp.where(row < HALO, row - HALO, row - HALO + rows)
    source = jnp.where((row < HALO - margin) | (row >= HALO + margin), -TILE - 1, source)
    cleared = jnp.zeros((TILE, features), jnp.bool_)
    for k in range(masks):
        offset = offsets_ref[k]
        first = first_of(offset)
        phase = offset & (BPT - 1)
        for side in range(2):
            here = row == edge + 2 * k + side
            token = first + side * spread
            seen = (token >= -margin) & (token < rows + margin)
            source = jnp.where(here, jnp.where(seen, token, -TILE - 1), source)
            hidden = column >= phase if side == 0 else column < phase
            cleared = cleared | (here & hidden)
    take = lax.broadcasted_iota(jnp.int32, (TILE, ext.shape[0]), 1) == source + TILE
    outer = jnp.dot(
        take.astype(jnp.float32).astype(jnp.bfloat16), ext, preferred_element_type=jnp.float32
    )
    outer = jnp.where(cleared, 0.0, outer).astype(jnp.bfloat16)
    emb_outer = jnp.dot(outer, stem[...], preferred_element_type=jnp.float32).astype(jnp.bfloat16)
    emb[0, rows:] = emb_outer
    x_b.start()
    core_b.start()
    emb_wide = emb_outer.astype(jnp.float32)
    emb_own[:HALO] = emb_wide[:HALO]
    emb_own[HALO + rows : past] = emb_wide[HALO:]
    conv(0, rows, rows + TILE)
    core_a.wait_recv()
    core_b.wait_recv()
    conv_copies[1].wait()
    conv(1, 0, rows + TILE)
    x_a.wait_recv()
    both_a.start()
    conv_copies[2].wait()
    conv(2, 0, ready)
    both_a.wait_recv()
    conv_copies[3].wait()
    conv(3, 0, ready)

    def trunk_rows(begin, count):
        begin = begin + HALO
        convolved = acc[0, pl.ds(begin - margin, count), :]
        for j in range(1, taps):
            convolved = convolved + acc[j, pl.ds(begin - margin + j, count), :]
        return emb_own[pl.ds(begin, count), :] + jax.nn.gelu(convolved)

    def window_rows(k, side):
        token = jnp.clip(
            first_of(offsets_ref[k]) + side * spread, -margin, rows + margin - 1
        ) + HALO
        own = HALO + rows + 2 + 2 * k + side
        step = lax.broadcasted_iota(jnp.int32, (GROUP, cols), 0)
        convolved = jnp.zeros((GROUP, cols), jnp.float32)
        center = jnp.where(step == margin, emb_own[own : own + 1, :], 0.0)
        for i in range(taps):
            total = acc[taps - 1 - i, own : own + 1, :]
            for j in range(taps):
                away = i + j - 2 * margin
                if away < 0 if side == 0 else away > 0:
                    total = total + acc[j, pl.ds(token + away, 1), :]
            convolved = jnp.where(step == i, total, convolved)
            away = i - margin
            if away < 0 if side == 0 else away > 0:
                center = jnp.where(step == i, emb_own[pl.ds(token + away, 1), :], center)
        return center + jax.nn.gelu(convolved)

    trunk[0, :EARLY] = trunk_rows(TILE, EARLY).astype(jnp.bfloat16)
    moves_t = gather(trunk, 1, (0, EARLY, trunk.shape[1]))
    moves_t[0][1].start()
    moves_t[0][0].start()
    x_b.wait_recv()
    both_b.start()
    conv(2, ready, rows + TILE)
    both_b.wait_recv()
    conv(3, ready, rows + TILE)
    late = [trunk_rows(0, TILE), trunk_rows(TILE + EARLY, rows - TILE - EARLY)]
    for k in range(masks):
        late += [window_rows(k, 0), window_rows(k, 1)]
    trunk[0, EARLY:] = jnp.concatenate(late, 0).astype(jnp.bfloat16)
    moves_t[1][1].start()
    moves_t[1][0].start()

    for copy in qkv_copies:
        copy.wait()

    def project(w, begin, end):
        by_core, by_x, by_both = moves_t[w]
        total = projected = None
        for r in range(4):
            if r == 1:
                by_core.wait_recv()
            if r == 2:
                by_x.wait_recv()
                by_both.start()
            if r == 3:
                by_both.wait_recv()
            block = trunk[r, begin:end]
            wide = block.astype(jnp.float32)
            square = jnp.sum(wide * wide, axis=1, keepdims=True)
            term = lax.dot_general(
                block, qw[r], (((1,), (1,)), ((), ())), preferred_element_type=jnp.float32
            )
            total = square if r == 0 else total + square
            projected = term if r == 0 else projected + term
        return (projected * lax.rsqrt(total / (4 * cols) + 1e-06)).astype(jnp.bfloat16)

    own_end = rows + TILE
    pieces = (
        (0, 48, 0, 48, 0),
        (48, EARLY, 48, EARLY - 48, 48),
        (EARLY, rows, EARLY, rows - EARLY, EARLY),
        (rows, rows + 2 * TILE, own_end, TILE, rows),
    )
    parts = len(pieces)

    def x_copy(shard, w):
        _, _, begin, count, to = pieces[w]
        n = shard * parts + w
        return remote(
            kv.at[shard, pl.ds(begin, count), :], kv_x.at[shard, pl.ds(to, count), :],
            x_send.at[n], x_recv.at[n], x_peer,
        )

    def z_copy(direction, w, shard, d):
        n = (direction * parts + w) * shards + d
        span = pl.ds(pieces[w][0], pieces[w][1] - pieces[w][0])
        return remote(
            kv.at[shard, span, :], kv.at[shard, span, :], z_send.at[n], z_recv.at[n],
            {"seq": s + (1 if direction == 0 else -1)},
        )

    def send_own(w):
        @pl.when(has_hi)
        def _():
            z_copy(0, w, s, 0).start()

        @pl.when(has_lo)
        def _():
            z_copy(1, w, s, 0).start()

        x_copy(s, w).start()

    def pass_on(w, d):
        @pl.when(s - d >= 0)
        def _():
            z_copy(0, w, s - d, d - 1).wait_recv()

        @pl.when((s - d >= 0) & has_hi)
        def _():
            z_copy(0, w, s - d, d).start()

        @pl.when(s - d >= 0)
        def _():
            x_copy(s - d, w).start()

        @pl.when(s + d < shards)
        def _():
            z_copy(1, w, s + d, d - 1).wait_recv()

        @pl.when((s + d < shards) & has_lo)
        def _():
            z_copy(1, w, s + d, d).start()

        @pl.when(s + d < shards)
        def _():
            x_copy(s + d, w).start()

    early = project(0, 0, EARLY)
    kv[s, :EARLY] = early[:, :wkv]
    send_own(0)
    send_own(1)
    qa[:EARLY] = early[:, wkv:]
    late = project(1, EARLY, trunk.shape[1])
    base_late = rows - EARLY
    kv[s, EARLY:rows] = late[:base_late, :wkv]
    send_own(2)
    two = late[base_late:, :wkv].astype(jnp.float32)
    zeroth = m == 0
    kv[s, rows:own_end] = jnp.where(zeroth, two[:TILE], two[TILE:]).astype(jnp.bfloat16)
    kv[s, own_end:] = jnp.where(zeroth, two[TILE:], two[:TILE]).astype(jnp.bfloat16)
    send_own(3)
    qa[EARLY:] = late[:, wkv:]

    def queries(k):
        first = first_of(offsets_ref[k])
        shape = (rows, qa.shape[0])
        token = lax.broadcasted_iota(jnp.int32, shape, 0)
        place = jnp.where(token < TILE, token + EARLY, token)
        place = jnp.where((token >= TILE) & (token < TILE + EARLY), token - TILE, place)
        begin = rows + k * TILE
        for side in range(2):
            step = token - first - side * spread + margin
            place = jnp.where(
                (step >= 0) & (step < taps), begin + side * GROUP + step, place
            )
        step = token - first
        place = jnp.where((step > margin) & (step < spread - margin), -1, place)
        pick = lax.broadcasted_iota(jnp.int32, shape, 1) == place
        return jnp.dot(
            pick.astype(jnp.float32).astype(jnp.bfloat16), qa[...],
            preferred_element_type=jnp.float32,
        ).astype(jnp.bfloat16)

    q_x[...] = queries(1 - m)
    q_to_x = remote(
        q_x, qs.at[1], x_send.at[shards * parts], x_recv.at[shards * parts], x_peer
    )
    q_to_x.start()
    qs[0] = queries(m)

    width = own_end
    tokens = shards * width
    key = lax.broadcasted_iota(jnp.int32, (1, tokens), 1)
    owner = jnp.zeros((1, tokens), jnp.int32)
    for d in range(1, shards):
        owner = owner + (key >= d * width).astype(jnp.int32)
    key = key - owner * width
    first = lax.shift_right_logical(offsets_ref[m], 7)
    local_token = jnp.where(key < EARLY, key + TILE, key)
    local_token = jnp.where((key >= EARLY) & (key < EARLY + TILE), key - EARLY, local_token)
    token = local_token + owner * rows - first
    kept_base = (key < rows) & ((token < -margin) | (token > spread + margin))
    slot = key - rows
    second = slot >= GROUP
    slot = jnp.where(second, slot - GROUP, slot)
    token = first - margin + slot + jnp.where(second, spread, 0) - owner * rows
    kept_window = (key >= rows) & (slot < taps) & (token >= 0) & (token < rows)
    bias = jnp.where(kept_base | kept_window, 0.0, -1e30)
    zero_tokens = spread - 2 * margin - 1

    for d in range(1, shards):
        for w in range(parts):
            pass_on(w, d)
    q_to_x.wait_recv()
    for d in range(shards):
        for w in range(parts):
            x_copy(d, w).wait_recv()

    lane = lax.broadcasted_iota(jnp.int32, (rows, qs.shape[2]), 1)
    scores = None
    keys_to = qs.shape[2]
    halves = (kv[:, :width, :].reshape(tokens, wkv), kv_x[...].reshape(tokens, wkv))
    for p in range(2):
        query = qs[p]
        zero = jnp.zeros_like(query)
        stack = jnp.concatenate(
            [jnp.where(lane < piece, query, zero), jnp.where(lane >= piece, query, zero)], 0
        )
        term = lax.dot_general(
            stack, halves[p][:, :keys_to], (((1,), (1,)), ((), ())),
            preferred_element_type=jnp.float32,
        )
        scores = term if scores is None else scores + term
    scores = scores * ((2 * piece) ** (-0.5)) + bias
    top = jnp.maximum(jnp.max(scores, axis=1, keepdims=True), 0.0)
    raised = jnp.exp(scores - top)
    denominator = jnp.sum(raised, axis=1, keepdims=True) + zero_tokens * jnp.exp(-top)
    weights = raised.astype(jnp.bfloat16)
    attended = []
    for p in range(2):
        value = halves[p][:, wkv - ow.shape[1] :]
        mixed = jnp.dot(weights, value, preferred_element_type=jnp.float32) / denominator
        at = lax.broadcasted_iota(jnp.int32, (rows, ow.shape[1]), 1)
        both = jnp.where(at < gap + piece, mixed[:rows], mixed[rows:])
        attended.append(jnp.where(at < gap, 0.0, both).astype(jnp.bfloat16))
    for copy in ow_copies:
        copy.wait()
    half = out_ref.shape[2]

    def share(side):
        where = pl.ds(pl.multiple_of(side * half, 128), half)
        return jnp.dot(
            attended[0], ow[0, :, where], preferred_element_type=jnp.float32
        ) + jnp.dot(attended[1], ow[1, :, where], preferred_element_type=jnp.float32)

    part_x[...] = share(1 - h).astype(jnp.bfloat16)
    swap = remote(part_x, part_in, p_sem.at[0], p_sem.at[1], core_peer)
    swap.start()
    kept = share(h)
    swap.wait_recv()
    out_ref[0] = (kept + part_in[...].astype(jnp.float32)).astype(jnp.bfloat16)

    swap.wait_send()
    for copy in (core_a, x_a, both_a, core_b, x_b, both_b, *moves_t[0], *moves_t[1], q_to_x):
        copy.wait_send()
    for d in range(shards):
        for w in range(parts):
            x_copy(d, w).wait_send()

    @pl.when(has_hi)
    def _():
        to_hi.wait_send()

    @pl.when(has_lo)
    def _():
        to_lo.wait_send()

    for d in range(shards - 1):
        for w in range(parts):
            @pl.when((s - d >= 0) & has_hi)
            def _(w=w, d=d):
                z_copy(0, w, s - d, d).wait_send()

            @pl.when((s + d < shards) & has_lo)
            def _(w=w, d=d):
                z_copy(1, w, s + d, d).wait_send()


def fused(shards, dna, offsets, stem_weight, conv_weight, qkv_weight, out_weight):
    rows, features = dna.shape
    cols = stem_weight.shape[1]
    taps = conv_weight.shape[0]
    depth = qkv_weight.shape[0]
    masks = offsets.shape[0]
    piece = qkv_weight.shape[3]
    width = out_weight.shape[1]
    wkv = 4 * piece
    query_pad = -(2 * piece) % 128
    qkv = jnp.transpose(qkv_weight, (1, 2, 3, 0)).reshape(6 * piece, depth)
    wq = 2 * piece + query_pad
    deep = wkv - (2 * piece // 128) * 128
    stack = rows + 2 * HALO
    trows = rows + masks * TILE
    bf, f32 = jnp.bfloat16, jnp.float32
    dma = pltpu.SemaphoreType.DMA
    anywhere = pl.BlockSpec(memory_space=pltpu.HBM)
    return pl.pallas_call(
        fused_kernel,
        out_shape=pltpu.VMEM((1, rows, width // 2), bf),
        in_specs=[
            pl.BlockSpec(memory_space=pltpu.SMEM),
            pl.BlockSpec(memory_space=pltpu.VMEM),
            anywhere, anywhere, anywhere, anywhere,
        ],
        out_specs=pl.BlockSpec(memory_space=pltpu.VMEM),
        scratch_shapes=[
            pltpu.VMEM((TILE, features), bf),
            pltpu.VMEM((TILE, features), bf),
            pltpu.VMEM((features, cols), bf),
            pltpu.VMEM((4, taps, cols, cols), bf),
            pltpu.VMEM((4, wkv + wq, cols), bf),
            pltpu.VMEM((2, deep, width), bf),
            pltpu.VMEM((4, rows + TILE, cols), bf),
            pltpu.VMEM((stack, cols), f32),
            pltpu.VMEM((taps, stack, cols), f32),
            pltpu.VMEM((4, trows, cols), bf),
            pltpu.VMEM((shards, trows, wkv), bf),
            pltpu.VMEM((shards, rows + TILE, wkv), bf),
            pltpu.VMEM((trows, wq), bf),
            pltpu.VMEM((2, rows, wq), bf),
            pltpu.VMEM((rows, wq), bf),
            pltpu.VMEM((rows, width // 2), bf),
            pltpu.VMEM((rows, width // 2), bf),
            dma((21,)),
            dma((2,)),
            dma((2,)),
            dma((12,)),
            dma((12,)),
            dma((4 * shards + 1,)),
            dma((4 * shards + 1,)),
            dma((8 * shards,)),
            dma((8 * shards,)),
            dma((2,)),
        ],
        compiler_params=pltpu.CompilerParams(
            collective_id=0, has_side_effects=True, vmem_limit_bytes=62 * 2**20
        ),
    )(offsets, dna, stem_weight, conv_weight, qkv, out_weight)


def solution(mesh):
    placed = (
        P(("grp", "seq"), None),
        P("grp"),
        P(None, ("mask", "head")),
        P(None, None, ("mask", "head")),
        P(None, None, "head", "mask"),
        P("head", None),
    )
    shape = mesh.shape

    def body(*arrays):
        piece, cols = arrays[4].shape[3], arrays[2].shape[1]
        fits = piece % 32 == 0 and cols % 128 == 0 and arrays[0].shape[0] >= EARLY + 2 * TILE
        if shape["mask"] == 2 and shape["head"] == 2 and arrays[1].shape[0] == 2 and fits:
            return fused(shape["seq"], *arrays)
        return local(*arrays)

    return jax.shard_map(
        body,
        mesh=mesh,
        in_specs=placed,
        out_specs=P(("grp", "mask"), "seq", "head"),
        check_vma=False,
    )
```

```python
import jax
import jax.numpy as jnp
from jax import lax
from jax.experimental import pallas as pl
from jax.experimental.pallas import tpu as pltpu
from jax.sharding import PartitionSpec as P

BPT = 128
MASK_DEV = 1
WIN_BP = 2048
WROWS = 24


def padded(cells, sides, width):
    for axis, dim in sides:
        count = lax.axis_size(axis)
        ends = count - 1
        head = lax.slice_in_dim(cells, 0, width, axis=dim)
        tail = lax.slice_in_dim(cells, cells.shape[dim] - width, cells.shape[dim], axis=dim)
        cells = jnp.concatenate(
            [
                lax.ppermute(tail, axis, [(i, (i + 1) % count) for i in range(ends)]),
                cells,
                lax.ppermute(head, axis, [((i + 1) % count, i) for i in range(ends)]),
            ],
            axis=dim,
        )
    return cells


def conv_rows(source, weight, out_rows):
    summed = None
    for kernel_tap in range(weight.shape[0]):
        tap_rows = lax.slice_in_dim(source, kernel_tap, kernel_tap + out_rows, axis=source.ndim - 2)
        tap_term = jnp.einsum(
            "...rc,cd->...rd", tap_rows, weight[kernel_tap], preferred_element_type=jnp.float32
        )
        summed = tap_term if summed is None else summed + tap_term
    return summed


def local(dna, offsets, stem_weight, conv_weight, qkv_weight, out_weight):
    tok_rows, features = dna.shape
    margin = conv_weight.shape[0] // 2
    row_start = lax.axis_index("seq") * tok_rows
    masks_all = offsets.shape[0]
    window_rows = WROWS
    span_rows = window_rows + 2 * margin
    extended = padded(dna, (("seq", 0),), margin)
    first_token = offsets // BPT
    local_start = jnp.clip(first_token - margin - row_start, 0, tok_rows - window_rows)

    def cut_window(window_begin):
        return lax.dynamic_slice_in_dim(extended, window_begin, span_rows, 0)

    window_dna = jax.vmap(cut_window)(local_start)
    row_steps = lax.iota(jnp.int32, span_rows)
    base_pair = lax.iota(jnp.int32, features) // 4
    positions = (
        row_start + local_start[:, None, None] - margin + row_steps[None, :, None]
    ) * BPT + base_pair[None, None, :]
    inside = (positions >= offsets[:, None, None]) & (positions < offsets[:, None, None] + WIN_BP)
    masked = jnp.where(inside, jnp.zeros_like(window_dna), window_dna)
    stacked = jnp.concatenate([extended, masked.reshape(masks_all * span_rows, features)], 0)
    embedded = jnp.dot(stacked, stem_weight, preferred_element_type=jnp.float32).astype(
        jnp.bfloat16
    )
    columns = embedded.shape[1]
    base_length = tok_rows + 2 * margin
    shard_part = lax.all_gather(embedded, ("mask", "head"), axis=1, tiled=True)
    part_width = shard_part.shape[1]
    base_out = conv_rows(shard_part[:base_length], conv_weight, tok_rows)
    window_part = shard_part[base_length:].reshape(masks_all, span_rows, part_width)
    window_out = conv_rows(window_part, conv_weight, window_rows)
    convolved = jnp.concatenate([base_out, window_out.reshape(masks_all * window_rows, columns)], 0)
    window_emb = embedded[base_length:].reshape(masks_all, span_rows, columns)[
        :, margin : margin + window_rows
    ]
    own_embedded = jnp.concatenate(
        [
            embedded[margin : margin + tok_rows],
            window_emb.reshape(masks_all * window_rows, columns),
        ],
        0,
    )
    trunk_part = (own_embedded.astype(jnp.float32) + jax.nn.gelu(convolved)).astype(jnp.bfloat16)
    trunk = lax.all_gather(trunk_part, ("mask", "head"), axis=1, tiled=True)
    width_all = trunk.shape[1]
    first_own = lax.axis_index("mask") * MASK_DEV
    own_windows = lax.dynamic_slice_in_dim(
        trunk[tok_rows:].reshape(masks_all, window_rows, width_all), first_own, MASK_DEV, 0
    )
    trunk_rows = jnp.concatenate(
        [trunk[:tok_rows], own_windows.reshape(MASK_DEV * window_rows, width_all)], 0
    )
    wide = trunk_rows.astype(jnp.float32)
    normed = (wide * lax.rsqrt(jnp.mean(wide * wide, axis=1, keepdims=True) + 1e-06)).astype(
        jnp.bfloat16
    )
    projected = jnp.einsum(
        "rd,dthc->rthc",
        normed,
        lax.all_gather(qkv_weight, "mask", axis=3, tiled=True),
        preferred_element_type=jnp.float32,
    ).astype(jnp.bfloat16)
    heads_here = projected.shape[2]
    head_size = projected.shape[3]
    base_qkv = projected[:tok_rows]
    window_qkv = projected[tok_rows:].reshape(MASK_DEV, window_rows, 3, heads_here, head_size)
    own_start = lax.dynamic_slice_in_dim(local_start, first_own, MASK_DEV, 0)
    scaling = head_size ** (-0.5)
    merged = lax.dynamic_update_slice_in_dim(base_qkv, window_qkv[0], own_start[0], 0)
    queries = merged[:, 0]
    running_top = jnp.full((heads_here, tok_rows), -1e30, jnp.float32)
    key_part = lax.all_gather(merged[:, 1], "seq", axis=0, tiled=True)
    value_part = lax.all_gather(merged[:, 2], "seq", axis=0, tiled=True)
    scores = (
        jnp.einsum("qhc,khc->hqk", queries, key_part, preferred_element_type=jnp.float32) * scaling
    )
    new_top = jnp.maximum(running_top, jnp.max(scores, axis=2))
    raised = jnp.exp(scores - new_top[:, :, None])
    denominator = jnp.sum(raised, axis=2)
    weighted = jnp.einsum(
        "hqk,khc->hqc", raised.astype(jnp.bfloat16), value_part, preferred_element_type=jnp.float32
    )
    running_top, denominator, weighted = (new_top, denominator, weighted)
    results = [weighted / denominator[:, :, None]]
    attended = jnp.stack(results).astype(jnp.bfloat16)
    attended = jnp.transpose(attended, (0, 2, 1, 3)).reshape(
        MASK_DEV, tok_rows, heads_here * head_size
    )
    partial_sums = jnp.einsum(
        "mqc,cd->mqd", attended, out_weight, preferred_element_type=jnp.float32
    )
    mixed = lax.psum_scatter(
        partial_sums.astype(jnp.bfloat16), "head", scatter_dimension=2, tiled=True
    )
    return mixed


MESH = pl.DeviceIdType.MESH
HALO = 8
TILE = 16
EARLY = 80
GROUP = 8


def fused_kernel(
    offsets_hbm, dna_hbm, stem_hbm, conv_hbm, qkv_hbm, ow_hbm, out_ref,
    offsets_ref, dna_ref, halo_lo, halo_hi, stem, cw, qw, ow, emb, emb_own, acc, trunk, kv, kv_x, qa, qs, q_x,
    part_x, part_in,
    w_sem, halo_send, halo_recv, ag_send, ag_recv, x_send, x_recv, z_send, z_recv, p_sem,
):
    rows, features = dna_ref.shape
    cols = stem.shape[1]
    piece = ow_hbm.shape[0] // 4
    wkv, nq = 4 * piece, 2 * piece
    shards = kv.shape[0]
    taps = cw.shape[1]
    margin = taps // 2
    spread = WIN_BP // BPT
    masks = offsets_ref.shape[0]
    m, h, s = lax.axis_index("mask"), lax.axis_index("head"), lax.axis_index("seq")
    row_start = s * rows
    core_peer = {"head": 1 - h}
    x_peer = {"mask": 1 - m}
    has_lo, has_hi = s > 0, s < shards - 1

    def remote(src, dst, send, recv, device):
        return pltpu.make_async_remote_copy(
            src_ref=src, dst_ref=dst, send_sem=send, recv_sem=recv,
            device_id=device, device_id_type=MESH,
        )

    barrier = pltpu.get_barrier_semaphore()
    for peer in (core_peer, x_peer):
        pl.semaphore_signal(barrier, inc=1, device_id=peer, device_id_type=MESH)

    @pl.when(has_lo)
    def _():
        pl.semaphore_signal(barrier, inc=1, device_id={"seq": s - 1}, device_id_type=MESH)

    @pl.when(has_hi)
    def _():
        pl.semaphore_signal(barrier, inc=1, device_id={"seq": s + 1}, device_id_type=MESH)

    slot_of = (2 * m + h, 2 * m + 1 - h, 2 * (1 - m) + h, 2 * (1 - m) + 1 - h)
    stem_copy = pltpu.make_async_copy(stem_hbm, stem, w_sem.at[0])
    dna_copy = pltpu.make_async_copy(dna_hbm, dna_ref, w_sem.at[21])
    dna_copy.start()
    off_copy = pltpu.make_async_copy(offsets_hbm, offsets_ref, w_sem.at[22])
    off_copy.start()
    stem_copy.start()
    conv_copies, qkv_copies, ow_copies = [], [], []
    for r in range(4):
        span = pl.ds(pl.multiple_of(slot_of[r] * cols, 128), cols)
        conv_copies.append(
            pltpu.make_async_copy(conv_hbm.at[:, span, :], cw.at[r], w_sem.at[1 + r])
        )
        conv_copies[r].start()
    for r in range(4):
        span = pl.ds(pl.multiple_of(slot_of[r] * cols, 128), cols)
        for k, (src, dst, count) in enumerate(((nq, 0, wkv), (0, wkv, nq))):
            copy = pltpu.make_async_copy(
                qkv_hbm.at[pl.ds(src, count), span],
                qw.at[r, pl.ds(dst, count), :],
                w_sem.at[13 + 2 * r + k],
            )
            copy.start()
            qkv_copies.append(copy)
    qw[:, wkv + nq :, :] = jnp.zeros((4, qw.shape[1] - wkv - nq, cols), qw.dtype)
    gap = ow.shape[1] - 2 * piece
    ow[:, 0:gap, :] = jnp.zeros((2, gap, ow.shape[2]), ow.dtype)
    for p, place in enumerate((m, 1 - m)):
        for hh in range(2):
            first = pl.multiple_of(hh * 2 * piece + place * piece, 16)
            copy = pltpu.make_async_copy(
                ow_hbm.at[pl.ds(first, piece), :],
                ow.at[p, pl.ds(gap + hh * piece, piece), :],
                w_sem.at[9 + 2 * p + hh],
            )
            copy.start()
            ow_copies.append(copy)
    past = HALO + rows + HALO
    dna_copy.wait()
    stem_copy.wait()
    emb_inner = jnp.dot(
        dna_ref[...], stem[...], preferred_element_type=jnp.float32
    ).astype(jnp.bfloat16)
    emb[0, :rows] = emb_inner
    emb_own[HALO : HALO + rows] = emb_inner.astype(jnp.float32)

    pl.semaphore_wait(barrier, 2 + has_lo.astype(jnp.int32) + has_hi.astype(jnp.int32))

    to_hi = remote(
        dna_ref.at[pl.ds(rows - TILE, TILE), :], halo_lo, halo_send.at[0], halo_recv.at[0],
        {"seq": s + 1},
    )
    to_lo = remote(
        dna_ref.at[pl.ds(0, TILE), :], halo_hi, halo_send.at[1], halo_recv.at[1], {"seq": s - 1}
    )

    @pl.when(has_hi)
    def _():
        to_hi.start()

    @pl.when(has_lo)
    def _():
        to_lo.start()

    def gather(buf, g, cuts):
        def pair(src, dst, where, k, device):
            n = 3 * (2 * g + where) + k
            span = pl.ds(cuts[where], cuts[where + 1] - cuts[where])
            return remote(
                buf.at[src, span, :], buf.at[dst, span, :], ag_send.at[n], ag_recv.at[n], device
            )

        return [
            (pair(0, 1, w, 0, core_peer), pair(0, 2, w, 1, x_peer), pair(2, 3, w, 2, core_peer))
            for w in range(2)
        ]

    ready = EARLY + 2 * TILE
    (core_a, x_a, both_a), (core_b, x_b, both_b) = gather(emb, 0, (0, ready, rows + TILE))
    x_a.start()
    core_a.start()

    @pl.when(jnp.logical_not(has_lo))
    def _():
        halo_lo[...] = jnp.zeros(halo_lo.shape, halo_lo.dtype)

    @pl.when(jnp.logical_not(has_hi))
    def _():
        halo_hi[...] = jnp.zeros(halo_hi.shape, halo_hi.dtype)

    def conv(r, begin, end):
        for j in range(taps):
            term = jnp.dot(emb[r, begin:end], cw[r, j], preferred_element_type=jnp.float32)
            inner = min(end, rows) - begin
            if inner > 0:
                where = slice(HALO + begin, HALO + begin + inner)
                acc[j, where] = term[:inner] if r == 0 else acc[j, where] + term[:inner]
            if end > rows:
                low, high = term[inner : inner + HALO], term[inner + HALO :]
                acc[j, :HALO] = low if r == 0 else acc[j, :HALO] + low
                where = slice(HALO + rows, past)
                acc[j, where] = high if r == 0 else acc[j, where] + high

    conv_copies[0].wait()
    conv(0, 0, rows)

    @pl.when(has_lo)
    def _():
        to_hi.wait_recv()

    @pl.when(has_hi)
    def _():
        to_lo.wait_recv()

    def first_of(offset):
        return lax.shift_right_logical(offset, 7) - row_start

    off_copy.wait()
    edge = HALO + 2
    ext = jnp.concatenate([halo_lo[...], dna_ref[...], halo_hi[...]], 0)
    row = lax.broadcasted_iota(jnp.int32, (TILE, 1), 0)
    column = lax.shift_right_logical(lax.broadcasted_iota(jnp.int32, (TILE, features), 1), 2)
    source = jnp.where(row < HALO, row - HALO, row - HALO + rows)
    source = jnp.where((row < HALO - margin) | (row >= HALO + margin), -TILE - 1, source)
    cleared = jnp.zeros((TILE, features), jnp.bool_)
    for k in range(masks):
        offset = offsets_ref[k]
        first = first_of(offset)
        phase = offset & (BPT - 1)
        for side in range(2):
            here = row == edge + 2 * k + side
            token = first + side * spread
            seen = (token >= -margin) & (token < rows + margin)
            source = jnp.where(here, jnp.where(seen, token, -TILE - 1), source)
            hidden = column >= phase if side == 0 else column < phase
            cleared = cleared | (here & hidden)
    take = lax.broadcasted_iota(jnp.int32, (TILE, ext.shape[0]), 1) == source + TILE
    outer = jnp.dot(
        take.astype(jnp.float32).astype(jnp.bfloat16), ext, preferred_element_type=jnp.float32
    )
    outer = jnp.where(cleared, 0.0, outer).astype(jnp.bfloat16)
    emb_outer = jnp.dot(outer, stem[...], preferred_element_type=jnp.float32).astype(jnp.bfloat16)
    emb[0, rows:] = emb_outer
    x_b.start()
    core_b.start()
    emb_wide = emb_outer.astype(jnp.float32)
    emb_own[:HALO] = emb_wide[:HALO]
    emb_own[HALO + rows : past] = emb_wide[HALO:]
    conv(0, rows, rows + TILE)
    core_a.wait_recv()
    core_b.wait_recv()
    conv_copies[1].wait()
    conv(1, 0, rows + TILE)
    x_a.wait_recv()
    both_a.start()
    conv_copies[2].wait()
    conv(2, 0, ready)
    both_a.wait_recv()
    conv_copies[3].wait()
    conv(3, 0, ready)

    def trunk_rows(begin, count):
        begin = begin + HALO
        convolved = acc[0, pl.ds(begin - margin, count), :]
        for j in range(1, taps):
            convolved = convolved + acc[j, pl.ds(begin - margin + j, count), :]
        return emb_own[pl.ds(begin, count), :] + jax.nn.gelu(convolved)

    def window_rows(k, side):
        token = jnp.clip(
            first_of(offsets_ref[k]) + side * spread, -margin, rows + margin - 1
        ) + HALO
        own = HALO + rows + 2 + 2 * k + side
        step = lax.broadcasted_iota(jnp.int32, (GROUP, cols), 0)
        convolved = jnp.zeros((GROUP, cols), jnp.float32)
        center = jnp.where(step == margin, emb_own[own : own + 1, :], 0.0)
        for i in range(taps):
            total = acc[taps - 1 - i, own : own + 1, :]
            for j in range(taps):
                away = i + j - 2 * margin
                if away < 0 if side == 0 else away > 0:
                    total = total + acc[j, pl.ds(token + away, 1), :]
            convolved = jnp.where(step == i, total, convolved)
            away = i - margin
            if away < 0 if side == 0 else away > 0:
                center = jnp.where(step == i, emb_own[pl.ds(token + away, 1), :], center)
        return center + jax.nn.gelu(convolved)

    trunk[0, :EARLY] = trunk_rows(TILE, EARLY).astype(jnp.bfloat16)
    moves_t = gather(trunk, 1, (0, EARLY, trunk.shape[1]))
    moves_t[0][1].start()
    moves_t[0][0].start()
    x_b.wait_recv()
    both_b.start()
    conv(2, ready, rows + TILE)
    both_b.wait_recv()
    conv(3, ready, rows + TILE)
    late = [trunk_rows(0, TILE), trunk_rows(TILE + EARLY, rows - TILE - EARLY)]
    for k in range(masks):
        late += [window_rows(k, 0), window_rows(k, 1)]
    trunk[0, EARLY:] = jnp.concatenate(late, 0).astype(jnp.bfloat16)
    moves_t[1][1].start()
    moves_t[1][0].start()

    for copy in qkv_copies:
        copy.wait()

    def project(w, begin, end):
        by_core, by_x, by_both = moves_t[w]
        total = projected = None
        for r in range(4):
            if r == 1:
                by_core.wait_recv()
            if r == 2:
                by_x.wait_recv()
                by_both.start()
            if r == 3:
                by_both.wait_recv()
            block = trunk[r, begin:end]
            wide = block.astype(jnp.float32)
            square = jnp.sum(wide * wide, axis=1, keepdims=True)
            term = lax.dot_general(
                block, qw[r], (((1,), (1,)), ((), ())), preferred_element_type=jnp.float32
            )
            total = square if r == 0 else total + square
            projected = term if r == 0 else projected + term
        return (projected * lax.rsqrt(total / (4 * cols) + 1e-06)).astype(jnp.bfloat16)

    own_end = rows + TILE
    pieces = (
        (0, 48, 0, 48, 0),
        (48, EARLY, 48, EARLY - 48, 48),
        (EARLY, rows, EARLY, rows - EARLY, EARLY),
        (rows, rows + 2 * TILE, own_end, TILE, rows),
    )
    parts = len(pieces)

    def x_copy(shard, w):
        _, _, begin, count, to = pieces[w]
        n = shard * parts + w
        return remote(
            kv.at[shard, pl.ds(begin, count), :], kv_x.at[shard, pl.ds(to, count), :],
            x_send.at[n], x_recv.at[n], x_peer,
        )

    def z_copy(direction, w, shard, d):
        n = (direction * parts + w) * shards + d
        span = pl.ds(pieces[w][0], pieces[w][1] - pieces[w][0])
        return remote(
            kv.at[shard, span, :], kv.at[shard, span, :], z_send.at[n], z_recv.at[n],
            {"seq": s + (1 if direction == 0 else -1)},
        )

    def send_own(w):
        @pl.when(has_hi)
        def _():
            z_copy(0, w, s, 0).start()

        @pl.when(has_lo)
        def _():
            z_copy(1, w, s, 0).start()

        x_copy(s, w).start()

    def pass_on(w, d):
        @pl.when(s - d >= 0)
        def _():
            z_copy(0, w, s - d, d - 1).wait_recv()

        @pl.when((s - d >= 0) & has_hi)
        def _():
            z_copy(0, w, s - d, d).start()

        @pl.when(s - d >= 0)
        def _():
            x_copy(s - d, w).start()

        @pl.when(s + d < shards)
        def _():
            z_copy(1, w, s + d, d - 1).wait_recv()

        @pl.when((s + d < shards) & has_lo)
        def _():
            z_copy(1, w, s + d, d).start()

        @pl.when(s + d < shards)
        def _():
            x_copy(s + d, w).start()

    early = project(0, 0, EARLY)
    kv[s, :EARLY] = early[:, :wkv]
    send_own(0)
    send_own(1)
    qa[:EARLY] = early[:, wkv:]
    late = project(1, EARLY, trunk.shape[1])
    base_late = rows - EARLY
    kv[s, EARLY:rows] = late[:base_late, :wkv]
    send_own(2)
    two = late[base_late:, :wkv].astype(jnp.float32)
    zeroth = m == 0
    kv[s, rows:own_end] = jnp.where(zeroth, two[:TILE], two[TILE:]).astype(jnp.bfloat16)
    kv[s, own_end:] = jnp.where(zeroth, two[TILE:], two[:TILE]).astype(jnp.bfloat16)
    send_own(3)
    qa[EARLY:] = late[:, wkv:]

    def queries(k):
        first = first_of(offsets_ref[k])
        shape = (rows, qa.shape[0])
        token = lax.broadcasted_iota(jnp.int32, shape, 0)
        place = jnp.where(token < TILE, token + EARLY, token)
        place = jnp.where((token >= TILE) & (token < TILE + EARLY), token - TILE, place)
        begin = rows + k * TILE
        for side in range(2):
            step = token - first - side * spread + margin
            place = jnp.where(
                (step >= 0) & (step < taps), begin + side * GROUP + step, place
            )
        step = token - first
        place = jnp.where((step > margin) & (step < spread - margin), -1, place)
        pick = lax.broadcasted_iota(jnp.int32, shape, 1) == place
        return jnp.dot(
            pick.astype(jnp.float32).astype(jnp.bfloat16), qa[...],
            preferred_element_type=jnp.float32,
        ).astype(jnp.bfloat16)

    q_x[...] = queries(1 - m)
    q_to_x = remote(
        q_x, qs.at[1], x_send.at[shards * parts], x_recv.at[shards * parts], x_peer
    )
    q_to_x.start()
    qs[0] = queries(m)

    width = own_end
    tokens = shards * width
    key = lax.broadcasted_iota(jnp.int32, (1, tokens), 1)
    owner = jnp.zeros((1, tokens), jnp.int32)
    for d in range(1, shards):
        owner = owner + (key >= d * width).astype(jnp.int32)
    key = key - owner * width
    first = lax.shift_right_logical(offsets_ref[m], 7)
    local_token = jnp.where(key < EARLY, key + TILE, key)
    local_token = jnp.where((key >= EARLY) & (key < EARLY + TILE), key - EARLY, local_token)
    token = local_token + owner * rows - first
    kept_base = (key < rows) & ((token < -margin) | (token > spread + margin))
    slot = key - rows
    second = slot >= GROUP
    slot = jnp.where(second, slot - GROUP, slot)
    token = first - margin + slot + jnp.where(second, spread, 0) - owner * rows
    kept_window = (key >= rows) & (slot < taps) & (token >= 0) & (token < rows)
    bias = jnp.where(kept_base | kept_window, 0.0, -1e30)
    zero_tokens = spread - 2 * margin - 1

    for d in range(1, shards):
        for w in range(parts):
            pass_on(w, d)
    q_to_x.wait_recv()
    for d in range(shards):
        for w in range(parts):
            x_copy(d, w).wait_recv()

    lane = lax.broadcasted_iota(jnp.int32, (rows, qs.shape[2]), 1)
    scores = None
    keys_to = qs.shape[2]
    halves = (kv[:, :width, :].reshape(tokens, wkv), kv_x[...].reshape(tokens, wkv))
    for p in range(2):
        query = qs[p]
        zero = jnp.zeros_like(query)
        stack = jnp.concatenate(
            [jnp.where(lane < piece, query, zero), jnp.where(lane >= piece, query, zero)], 0
        )
        term = lax.dot_general(
            stack, halves[p][:, :keys_to], (((1,), (1,)), ((), ())),
            preferred_element_type=jnp.float32,
        )
        scores = term if scores is None else scores + term
    scores = scores * ((2 * piece) ** (-0.5)) + bias
    top = jnp.maximum(jnp.max(scores, axis=1, keepdims=True), 0.0)
    raised = jnp.exp(scores - top)
    denominator = jnp.sum(raised, axis=1, keepdims=True) + zero_tokens * jnp.exp(-top)
    weights = raised.astype(jnp.bfloat16)
    attended = []
    for p in range(2):
        value = halves[p][:, wkv - ow.shape[1] :]
        mixed = jnp.dot(weights, value, preferred_element_type=jnp.float32) / denominator
        at = lax.broadcasted_iota(jnp.int32, (rows, ow.shape[1]), 1)
        both = jnp.where(at < gap + piece, mixed[:rows], mixed[rows:])
        attended.append(jnp.where(at < gap, 0.0, both).astype(jnp.bfloat16))
    for copy in ow_copies:
        copy.wait()
    half = out_ref.shape[2]

    def share(side):
        where = pl.ds(pl.multiple_of(side * half, 128), half)
        return jnp.dot(
            attended[0], ow[0, :, where], preferred_element_type=jnp.float32
        ) + jnp.dot(attended[1], ow[1, :, where], preferred_element_type=jnp.float32)

    part_x[...] = share(1 - h).astype(jnp.bfloat16)
    swap = remote(part_x, part_in, p_sem.at[0], p_sem.at[1], core_peer)
    swap.start()
    kept = share(h)
    swap.wait_recv()
    out_ref[0] = (kept + part_in[...].astype(jnp.float32)).astype(jnp.bfloat16)

    swap.wait_send()
    for copy in (core_a, x_a, both_a, core_b, x_b, both_b, *moves_t[0], *moves_t[1], q_to_x):
        copy.wait_send()
    for d in range(shards):
        for w in range(parts):
            x_copy(d, w).wait_send()

    @pl.when(has_hi)
    def _():
        to_hi.wait_send()

    @pl.when(has_lo)
    def _():
        to_lo.wait_send()

    for d in range(shards - 1):
        for w in range(parts):
            @pl.when((s - d >= 0) & has_hi)
            def _(w=w, d=d):
                z_copy(0, w, s - d, d).wait_send()

            @pl.when((s + d < shards) & has_lo)
            def _(w=w, d=d):
                z_copy(1, w, s + d, d).wait_send()


def fused(shards, dna, offsets, stem_weight, conv_weight, qkv_weight, out_weight):
    rows, features = dna.shape
    cols = stem_weight.shape[1]
    taps = conv_weight.shape[0]
    depth = qkv_weight.shape[0]
    masks = offsets.shape[0]
    piece = qkv_weight.shape[3]
    width = out_weight.shape[1]
    wkv = 4 * piece
    query_pad = -(2 * piece) % 128
    qkv = jnp.transpose(qkv_weight, (1, 2, 3, 0)).reshape(6 * piece, depth)
    wq = 2 * piece + query_pad
    deep = wkv - (2 * piece // 128) * 128
    stack = rows + 2 * HALO
    trows = rows + masks * TILE
    bf, f32 = jnp.bfloat16, jnp.float32
    dma = pltpu.SemaphoreType.DMA
    anywhere = pl.BlockSpec(memory_space=pltpu.HBM)
    return pl.pallas_call(
        fused_kernel,
        out_shape=pltpu.VMEM((1, rows, width // 2), bf),
        in_specs=[
            anywhere, anywhere, anywhere, anywhere, anywhere, anywhere,
        ],
        out_specs=pl.BlockSpec(memory_space=pltpu.VMEM),
        scratch_shapes=[
            pltpu.SMEM((masks,), jnp.int32),
            pltpu.VMEM((rows, features), bf),
            pltpu.VMEM((TILE, features), bf),
            pltpu.VMEM((TILE, features), bf),
            pltpu.VMEM((features, cols), bf),
            pltpu.VMEM((4, taps, cols, cols), bf),
            pltpu.VMEM((4, wkv + wq, cols), bf),
            pltpu.VMEM((2, deep, width), bf),
            pltpu.VMEM((4, rows + TILE, cols), bf),
            pltpu.VMEM((stack, cols), f32),
            pltpu.VMEM((taps, stack, cols), f32),
            pltpu.VMEM((4, trows, cols), bf),
            pltpu.VMEM((shards, trows, wkv), bf),
            pltpu.VMEM((shards, rows + TILE, wkv), bf),
            pltpu.VMEM((trows, wq), bf),
            pltpu.VMEM((2, rows, wq), bf),
            pltpu.VMEM((rows, wq), bf),
            pltpu.VMEM((rows, width // 2), bf),
            pltpu.VMEM((rows, width // 2), bf),
            dma((23,)),
            dma((2,)),
            dma((2,)),
            dma((12,)),
            dma((12,)),
            dma((4 * shards + 1,)),
            dma((4 * shards + 1,)),
            dma((8 * shards,)),
            dma((8 * shards,)),
            dma((2,)),
        ],
        compiler_params=pltpu.CompilerParams(
            collective_id=0, has_side_effects=True, vmem_limit_bytes=62 * 2**20
        ),
    )(offsets, dna, stem_weight, conv_weight, qkv, out_weight)


def solution(mesh):
    placed = (
        P(("grp", "seq"), None),
        P("grp"),
        P(None, ("mask", "head")),
        P(None, None, ("mask", "head")),
        P(None, None, "head", "mask"),
        P("head", None),
    )
    shape = mesh.shape

    def body(*arrays):
        piece, cols = arrays[4].shape[3], arrays[2].shape[1]
        fits = piece % 32 == 0 and cols % 128 == 0 and arrays[0].shape[0] >= EARLY + 2 * TILE
        if shape["mask"] == 2 and shape["head"] == 2 and arrays[1].shape[0] == 2 and fits:
            return fused(shape["seq"], *arrays)
        return local(*arrays)

    return jax.shard_map(
        body,
        mesh=mesh,
        in_specs=placed,
        out_specs=P(("grp", "mask"), "seq", "head"),
        check_vma=False,
    )
```

```python
import jax
import jax.numpy as jnp
from jax import lax
from jax.experimental import pallas as pl
from jax.experimental.pallas import tpu as pltpu
from jax.sharding import PartitionSpec as P

BPT = 128
MASK_DEV = 1
WIN_BP = 2048
WROWS = 24


def padded(cells, sides, width):
    for axis, dim in sides:
        count = lax.axis_size(axis)
        ends = count - 1
        head = lax.slice_in_dim(cells, 0, width, axis=dim)
        tail = lax.slice_in_dim(cells, cells.shape[dim] - width, cells.shape[dim], axis=dim)
        cells = jnp.concatenate(
            [
                lax.ppermute(tail, axis, [(i, (i + 1) % count) for i in range(ends)]),
                cells,
                lax.ppermute(head, axis, [((i + 1) % count, i) for i in range(ends)]),
            ],
            axis=dim,
        )
    return cells


def conv_rows(source, weight, out_rows):
    summed = None
    for kernel_tap in range(weight.shape[0]):
        tap_rows = lax.slice_in_dim(source, kernel_tap, kernel_tap + out_rows, axis=source.ndim - 2)
        tap_term = jnp.einsum(
            "...rc,cd->...rd", tap_rows, weight[kernel_tap], preferred_element_type=jnp.float32
        )
        summed = tap_term if summed is None else summed + tap_term
    return summed


def local(dna, offsets, stem_weight, conv_weight, qkv_weight, out_weight):
    tok_rows, features = dna.shape
    margin = conv_weight.shape[0] // 2
    row_start = lax.axis_index("seq") * tok_rows
    masks_all = offsets.shape[0]
    window_rows = WROWS
    span_rows = window_rows + 2 * margin
    extended = padded(dna, (("seq", 0),), margin)
    first_token = offsets // BPT
    local_start = jnp.clip(first_token - margin - row_start, 0, tok_rows - window_rows)

    def cut_window(window_begin):
        return lax.dynamic_slice_in_dim(extended, window_begin, span_rows, 0)

    window_dna = jax.vmap(cut_window)(local_start)
    row_steps = lax.iota(jnp.int32, span_rows)
    base_pair = lax.iota(jnp.int32, features) // 4
    positions = (
        row_start + local_start[:, None, None] - margin + row_steps[None, :, None]
    ) * BPT + base_pair[None, None, :]
    inside = (positions >= offsets[:, None, None]) & (positions < offsets[:, None, None] + WIN_BP)
    masked = jnp.where(inside, jnp.zeros_like(window_dna), window_dna)
    stacked = jnp.concatenate([extended, masked.reshape(masks_all * span_rows, features)], 0)
    embedded = jnp.dot(stacked, stem_weight, preferred_element_type=jnp.float32).astype(
        jnp.bfloat16
    )
    columns = embedded.shape[1]
    base_length = tok_rows + 2 * margin
    shard_part = lax.all_gather(embedded, ("mask", "head"), axis=1, tiled=True)
    part_width = shard_part.shape[1]
    base_out = conv_rows(shard_part[:base_length], conv_weight, tok_rows)
    window_part = shard_part[base_length:].reshape(masks_all, span_rows, part_width)
    window_out = conv_rows(window_part, conv_weight, window_rows)
    convolved = jnp.concatenate([base_out, window_out.reshape(masks_all * window_rows, columns)], 0)
    window_emb = embedded[base_length:].reshape(masks_all, span_rows, columns)[
        :, margin : margin + window_rows
    ]
    own_embedded = jnp.concatenate(
        [
            embedded[margin : margin + tok_rows],
            window_emb.reshape(masks_all * window_rows, columns),
        ],
        0,
    )
    trunk_part = (own_embedded.astype(jnp.float32) + jax.nn.gelu(convolved)).astype(jnp.bfloat16)
    trunk = lax.all_gather(trunk_part, ("mask", "head"), axis=1, tiled=True)
    width_all = trunk.shape[1]
    first_own = lax.axis_index("mask") * MASK_DEV
    own_windows = lax.dynamic_slice_in_dim(
        trunk[tok_rows:].reshape(masks_all, window_rows, width_all), first_own, MASK_DEV, 0
    )
    trunk_rows = jnp.concatenate(
        [trunk[:tok_rows], own_windows.reshape(MASK_DEV * window_rows, width_all)], 0
    )
    wide = trunk_rows.astype(jnp.float32)
    normed = (wide * lax.rsqrt(jnp.mean(wide * wide, axis=1, keepdims=True) + 1e-06)).astype(
        jnp.bfloat16
    )
    projected = jnp.einsum(
        "rd,dthc->rthc",
        normed,
        lax.all_gather(qkv_weight, "mask", axis=3, tiled=True),
        preferred_element_type=jnp.float32,
    ).astype(jnp.bfloat16)
    heads_here = projected.shape[2]
    head_size = projected.shape[3]
    base_qkv = projected[:tok_rows]
    window_qkv = projected[tok_rows:].reshape(MASK_DEV, window_rows, 3, heads_here, head_size)
    own_start = lax.dynamic_slice_in_dim(local_start, first_own, MASK_DEV, 0)
    scaling = head_size ** (-0.5)
    merged = lax.dynamic_update_slice_in_dim(base_qkv, window_qkv[0], own_start[0], 0)
    queries = merged[:, 0]
    running_top = jnp.full((heads_here, tok_rows), -1e30, jnp.float32)
    key_part = lax.all_gather(merged[:, 1], "seq", axis=0, tiled=True)
    value_part = lax.all_gather(merged[:, 2], "seq", axis=0, tiled=True)
    scores = (
        jnp.einsum("qhc,khc->hqk", queries, key_part, preferred_element_type=jnp.float32) * scaling
    )
    new_top = jnp.maximum(running_top, jnp.max(scores, axis=2))
    raised = jnp.exp(scores - new_top[:, :, None])
    denominator = jnp.sum(raised, axis=2)
    weighted = jnp.einsum(
        "hqk,khc->hqc", raised.astype(jnp.bfloat16), value_part, preferred_element_type=jnp.float32
    )
    running_top, denominator, weighted = (new_top, denominator, weighted)
    results = [weighted / denominator[:, :, None]]
    attended = jnp.stack(results).astype(jnp.bfloat16)
    attended = jnp.transpose(attended, (0, 2, 1, 3)).reshape(
        MASK_DEV, tok_rows, heads_here * head_size
    )
    partial_sums = jnp.einsum(
        "mqc,cd->mqd", attended, out_weight, preferred_element_type=jnp.float32
    )
    mixed = lax.psum_scatter(
        partial_sums.astype(jnp.bfloat16), "head", scatter_dimension=2, tiled=True
    )
    return mixed


MESH = pl.DeviceIdType.MESH
HALO = 8
TILE = 16
EARLY = 96
GROUP = 8


def fused_kernel(
    offsets_hbm, dna_hbm, stem_hbm, conv_hbm, qkv_hbm, ow_hbm, out_ref,
    offsets_ref, dna_ref, halo_lo, halo_hi, stem, cw, qw, ow, emb, emb_own, acc, trunk, kv, kv_x, qa, qs, q_x,
    part_x, part_in,
    w_sem, halo_send, halo_recv, ag_send, ag_recv, x_send, x_recv, z_send, z_recv, p_sem,
):
    rows, features = dna_ref.shape
    cols = stem.shape[1]
    piece = ow_hbm.shape[0] // 4
    wkv, nq = 4 * piece, 2 * piece
    shards = kv.shape[0]
    taps = cw.shape[1]
    margin = taps // 2
    spread = WIN_BP // BPT
    masks = offsets_ref.shape[0]
    m, h, s = lax.axis_index("mask"), lax.axis_index("head"), lax.axis_index("seq")
    row_start = s * rows
    core_peer = {"head": 1 - h}
    x_peer = {"mask": 1 - m}
    cross_peer = {"mask": 1 - m, "head": 1 - h}
    has_lo, has_hi = s > 0, s < shards - 1

    def remote(src, dst, send, recv, device):
        return pltpu.make_async_remote_copy(
            src_ref=src, dst_ref=dst, send_sem=send, recv_sem=recv,
            device_id=device, device_id_type=MESH,
        )

    barrier = pltpu.get_barrier_semaphore()
    for peer in (core_peer, x_peer, cross_peer):
        pl.semaphore_signal(barrier, inc=1, device_id=peer, device_id_type=MESH)

    @pl.when(has_lo)
    def _():
        pl.semaphore_signal(barrier, inc=1, device_id={"seq": s - 1}, device_id_type=MESH)

    @pl.when(has_hi)
    def _():
        pl.semaphore_signal(barrier, inc=1, device_id={"seq": s + 1}, device_id_type=MESH)

    slot_of = (2 * m + h, 2 * m + 1 - h, 2 * (1 - m) + 1 - h, 2 * (1 - m) + h)
    stem_copy = pltpu.make_async_copy(stem_hbm, stem, w_sem.at[0])
    dna_copy = pltpu.make_async_copy(dna_hbm, dna_ref, w_sem.at[21])
    dna_copy.start()
    off_copy = pltpu.make_async_copy(offsets_hbm, offsets_ref, w_sem.at[22])
    off_copy.start()
    stem_copy.start()
    conv_copies, qkv_copies, ow_copies = [], [], []
    for r in range(4):
        span = pl.ds(pl.multiple_of(slot_of[r] * cols, 128), cols)
        conv_copies.append(
            pltpu.make_async_copy(conv_hbm.at[:, span, :], cw.at[r], w_sem.at[1 + r])
        )
        conv_copies[r].start()
    for r in range(4):
        span = pl.ds(pl.multiple_of(slot_of[r] * cols, 128), cols)
        for k, (src, dst, count) in enumerate(((nq, 0, wkv), (0, wkv, nq))):
            copy = pltpu.make_async_copy(
                qkv_hbm.at[pl.ds(src, count), span],
                qw.at[r, pl.ds(dst, count), :],
                w_sem.at[13 + 2 * r + k],
            )
            copy.start()
            qkv_copies.append(copy)
    qw[:, wkv + nq :, :] = jnp.zeros((4, qw.shape[1] - wkv - nq, cols), qw.dtype)
    gap = ow.shape[1] - 2 * piece
    ow[:, 0:gap, :] = jnp.zeros((2, gap, ow.shape[2]), ow.dtype)
    for p, place in enumerate((m, 1 - m)):
        for hh in range(2):
            first = pl.multiple_of(hh * 2 * piece + place * piece, 16)
            copy = pltpu.make_async_copy(
                ow_hbm.at[pl.ds(first, piece), :],
                ow.at[p, pl.ds(gap + hh * piece, piece), :],
                w_sem.at[9 + 2 * p + hh],
            )
            copy.start()
            ow_copies.append(copy)
    past = HALO + rows + HALO
    dna_copy.wait()
    stem_copy.wait()
    emb_inner = jnp.dot(
        dna_ref[...], stem[...], preferred_element_type=jnp.float32
    ).astype(jnp.bfloat16)
    emb[0, :rows] = emb_inner
    emb_own[HALO : HALO + rows] = emb_inner.astype(jnp.float32)

    pl.semaphore_wait(barrier, 3 + has_lo.astype(jnp.int32) + has_hi.astype(jnp.int32))

    to_hi = remote(
        dna_ref.at[pl.ds(rows - TILE, TILE), :], halo_lo, halo_send.at[0], halo_recv.at[0],
        {"seq": s + 1},
    )
    to_lo = remote(
        dna_ref.at[pl.ds(0, TILE), :], halo_hi, halo_send.at[1], halo_recv.at[1], {"seq": s - 1}
    )

    @pl.when(has_hi)
    def _():
        to_hi.start()

    @pl.when(has_lo)
    def _():
        to_lo.start()

    def gather(buf, g, cuts):
        def pair(src, dst, where, k, device):
            n = 3 * (2 * g + where) + k
            span = pl.ds(cuts[where], cuts[where + 1] - cuts[where])
            return remote(
                buf.at[src, span, :], buf.at[dst, span, :], ag_send.at[n], ag_recv.at[n], device
            )

        return [
            (pair(0, 1, w, 0, core_peer), pair(0, 2, w, 1, cross_peer), pair(2, 3, w, 2, core_peer))
            for w in range(2)
        ]

    ready = EARLY + 2 * TILE
    (core_a, x_a, both_a), (core_b, x_b, both_b) = gather(emb, 0, (0, ready, rows + TILE))
    x_a.start()
    core_a.start()

    @pl.when(jnp.logical_not(has_lo))
    def _():
        halo_lo[...] = jnp.zeros(halo_lo.shape, halo_lo.dtype)

    @pl.when(jnp.logical_not(has_hi))
    def _():
        halo_hi[...] = jnp.zeros(halo_hi.shape, halo_hi.dtype)

    def conv(r, begin, end):
        for j in range(taps):
            term = jnp.dot(emb[r, begin:end], cw[r, j], preferred_element_type=jnp.float32)
            inner = min(end, rows) - begin
            if inner > 0:
                where = slice(HALO + begin, HALO + begin + inner)
                acc[j, where] = term[:inner] if r == 0 else acc[j, where] + term[:inner]
            if end > rows:
                low, high = term[inner : inner + HALO], term[inner + HALO :]
                acc[j, :HALO] = low if r == 0 else acc[j, :HALO] + low
                where = slice(HALO + rows, past)
                acc[j, where] = high if r == 0 else acc[j, where] + high

    conv_copies[0].wait()
    conv(0, 0, rows)

    @pl.when(has_lo)
    def _():
        to_hi.wait_recv()

    @pl.when(has_hi)
    def _():
        to_lo.wait_recv()

    def first_of(offset):
        return lax.shift_right_logical(offset, 7) - row_start

    off_copy.wait()
    edge = HALO + 2
    ext = jnp.concatenate([halo_lo[...], dna_ref[...], halo_hi[...]], 0)
    row = lax.broadcasted_iota(jnp.int32, (TILE, 1), 0)
    column = lax.shift_right_logical(lax.broadcasted_iota(jnp.int32, (TILE, features), 1), 2)
    source = jnp.where(row < HALO, row - HALO, row - HALO + rows)
    source = jnp.where((row < HALO - margin) | (row >= HALO + margin), -TILE - 1, source)
    cleared = jnp.zeros((TILE, features), jnp.bool_)
    for k in range(masks):
        offset = offsets_ref[k]
        first = first_of(offset)
        phase = offset & (BPT - 1)
        for side in range(2):
            here = row == edge + 2 * k + side
            token = first + side * spread
            seen = (token >= -margin) & (token < rows + margin)
            source = jnp.where(here, jnp.where(seen, token, -TILE - 1), source)
            hidden = column >= phase if side == 0 else column < phase
            cleared = cleared | (here & hidden)
    take = lax.broadcasted_iota(jnp.int32, (TILE, ext.shape[0]), 1) == source + TILE
    outer = jnp.dot(
        take.astype(jnp.float32).astype(jnp.bfloat16), ext, preferred_element_type=jnp.float32
    )
    outer = jnp.where(cleared, 0.0, outer).astype(jnp.bfloat16)
    emb_outer = jnp.dot(outer, stem[...], preferred_element_type=jnp.float32).astype(jnp.bfloat16)
    emb[0, rows:] = emb_outer
    x_b.start()
    core_b.start()
    emb_wide = emb_outer.astype(jnp.float32)
    emb_own[:HALO] = emb_wide[:HALO]
    emb_own[HALO + rows : past] = emb_wide[HALO:]
    conv(0, rows, rows + TILE)
    core_a.wait_recv()
    core_b.wait_recv()
    conv_copies[1].wait()
    conv(1, 0, rows + TILE)
    x_a.wait_recv()
    both_a.start()
    conv_copies[2].wait()
    conv(2, 0, ready)
    both_a.wait_recv()
    conv_copies[3].wait()
    conv(3, 0, ready)

    def trunk_rows(begin, count):
        begin = begin + HALO
        convolved = acc[0, pl.ds(begin - margin, count), :]
        for j in range(1, taps):
            convolved = convolved + acc[j, pl.ds(begin - margin + j, count), :]
        return emb_own[pl.ds(begin, count), :] + jax.nn.gelu(convolved)

    def window_rows(k, side):
        token = jnp.clip(
            first_of(offsets_ref[k]) + side * spread, -margin, rows + margin - 1
        ) + HALO
        own = HALO + rows + 2 + 2 * k + side
        step = lax.broadcasted_iota(jnp.int32, (GROUP, cols), 0)
        convolved = jnp.zeros((GROUP, cols), jnp.float32)
        center = jnp.where(step == margin, emb_own[own : own + 1, :], 0.0)
        for i in range(taps):
            total = acc[taps - 1 - i, own : own + 1, :]
            for j in range(taps):
                away = i + j - 2 * margin
                if away < 0 if side == 0 else away > 0:
                    total = total + acc[j, pl.ds(token + away, 1), :]
            convolved = jnp.where(step == i, total, convolved)
            away = i - margin
            if away < 0 if side == 0 else away > 0:
                center = jnp.where(step == i, emb_own[pl.ds(token + away, 1), :], center)
        return center + jax.nn.gelu(convolved)

    trunk[0, :EARLY] = trunk_rows(TILE, EARLY).astype(jnp.bfloat16)
    moves_t = gather(trunk, 1, (0, EARLY, trunk.shape[1]))
    moves_t[0][1].start()
    moves_t[0][0].start()
    x_b.wait_recv()
    both_b.start()
    conv(2, ready, rows + TILE)
    both_b.wait_recv()
    conv(3, ready, rows + TILE)
    late = [trunk_rows(0, TILE), trunk_rows(TILE + EARLY, rows - TILE - EARLY)]
    for k in range(masks):
        late += [window_rows(k, 0), window_rows(k, 1)]
    trunk[0, EARLY:] = jnp.concatenate(late, 0).astype(jnp.bfloat16)
    moves_t[1][1].start()
    moves_t[1][0].start()

    for copy in qkv_copies:
        copy.wait()

    def project(w, begin, end):
        by_core, by_x, by_both = moves_t[w]
        total = projected = None
        for r in range(4):
            if r == 1:
                by_core.wait_recv()
            if r == 2:
                by_x.wait_recv()
                by_both.start()
            if r == 3:
                by_both.wait_recv()
            block = trunk[r, begin:end]
            wide = block.astype(jnp.float32)
            square = jnp.sum(wide * wide, axis=1, keepdims=True)
            term = lax.dot_general(
                block, qw[r], (((1,), (1,)), ((), ())), preferred_element_type=jnp.float32
            )
            total = square if r == 0 else total + square
            projected = term if r == 0 else projected + term
        return (projected * lax.rsqrt(total / (4 * cols) + 1e-06)).astype(jnp.bfloat16)

    own_end = rows + TILE
    pieces = (
        (0, 48, 0, 48, 0),
        (48, EARLY, 48, EARLY - 48, 48),
        (EARLY, rows, EARLY, rows - EARLY, EARLY),
        (rows, rows + 2 * TILE, own_end, TILE, rows),
    )
    parts = len(pieces)

    def x_copy(shard, w):
        _, _, begin, count, to = pieces[w]
        n = shard * parts + w
        return remote(
            kv.at[shard, pl.ds(begin, count), :], kv_x.at[shard, pl.ds(to, count), :],
            x_send.at[n], x_recv.at[n], x_peer,
        )

    def z_copy(direction, w, shard, d):
        n = (direction * parts + w) * shards + d
        span = pl.ds(pieces[w][0], pieces[w][1] - pieces[w][0])
        return remote(
            kv.at[shard, span, :], kv.at[shard, span, :], z_send.at[n], z_recv.at[n],
            {"seq": s + (1 if direction == 0 else -1)},
        )

    def send_own(w):
        @pl.when(has_hi)
        def _():
            z_copy(0, w, s, 0).start()

        @pl.when(has_lo)
        def _():
            z_copy(1, w, s, 0).start()

        x_copy(s, w).start()

    def pass_on(w, d):
        @pl.when(s - d >= 0)
        def _():
            z_copy(0, w, s - d, d - 1).wait_recv()

        @pl.when((s - d >= 0) & has_hi)
        def _():
            z_copy(0, w, s - d, d).start()

        @pl.when(s - d >= 0)
        def _():
            x_copy(s - d, w).start()

        @pl.when(s + d < shards)
        def _():
            z_copy(1, w, s + d, d - 1).wait_recv()

        @pl.when((s + d < shards) & has_lo)
        def _():
            z_copy(1, w, s + d, d).start()

        @pl.when(s + d < shards)
        def _():
            x_copy(s + d, w).start()

    early = project(0, 0, EARLY)
    kv[s, :EARLY] = early[:, :wkv]
    send_own(0)
    send_own(1)
    qa[:EARLY] = early[:, wkv:]
    late = project(1, EARLY, trunk.shape[1])
    base_late = rows - EARLY
    kv[s, EARLY:rows] = late[:base_late, :wkv]
    send_own(2)
    two = late[base_late:, :wkv].astype(jnp.float32)
    zeroth = m == 0
    kv[s, rows:own_end] = jnp.where(zeroth, two[:TILE], two[TILE:]).astype(jnp.bfloat16)
    kv[s, own_end:] = jnp.where(zeroth, two[TILE:], two[:TILE]).astype(jnp.bfloat16)
    send_own(3)
    qa[EARLY:] = late[:, wkv:]

    def queries(k):
        first = first_of(offsets_ref[k])
        shape = (rows, qa.shape[0])
        token = lax.broadcasted_iota(jnp.int32, shape, 0)
        place = jnp.where(token < TILE, token + EARLY, token)
        place = jnp.where((token >= TILE) & (token < TILE + EARLY), token - TILE, place)
        begin = rows + k * TILE
        for side in range(2):
            step = token - first - side * spread + margin
            place = jnp.where(
                (step >= 0) & (step < taps), begin + side * GROUP + step, place
            )
        step = token - first
        place = jnp.where((step > margin) & (step < spread - margin), -1, place)
        pick = lax.broadcasted_iota(jnp.int32, shape, 1) == place
        return jnp.dot(
            pick.astype(jnp.float32).astype(jnp.bfloat16), qa[...],
            preferred_element_type=jnp.float32,
        ).astype(jnp.bfloat16)

    q_x[...] = queries(1 - m)
    q_to_x = remote(
        q_x, qs.at[1], x_send.at[shards * parts], x_recv.at[shards * parts], x_peer
    )
    q_to_x.start()
    qs[0] = queries(m)

    width = own_end
    tokens = shards * width
    key = lax.broadcasted_iota(jnp.int32, (1, tokens), 1)
    owner = jnp.zeros((1, tokens), jnp.int32)
    for d in range(1, shards):
        owner = owner + (key >= d * width).astype(jnp.int32)
    key = key - owner * width
    first = lax.shift_right_logical(offsets_ref[m], 7)
    local_token = jnp.where(key < EARLY, key + TILE, key)
    local_token = jnp.where((key >= EARLY) & (key < EARLY + TILE), key - EARLY, local_token)
    token = local_token + owner * rows - first
    kept_base = (key < rows) & ((token < -margin) | (token > spread + margin))
    slot = key - rows
    second = slot >= GROUP
    slot = jnp.where(second, slot - GROUP, slot)
    token = first - margin + slot + jnp.where(second, spread, 0) - owner * rows
    kept_window = (key >= rows) & (slot < taps) & (token >= 0) & (token < rows)
    bias = jnp.where(kept_base | kept_window, 0.0, -1e30)
    zero_tokens = spread - 2 * margin - 1

    for d in range(1, shards):
        for w in range(parts):
            pass_on(w, d)
    q_to_x.wait_recv()
    for d in range(shards):
        for w in range(parts):
            x_copy(d, w).wait_recv()

    lane = lax.broadcasted_iota(jnp.int32, (rows, qs.shape[2]), 1)
    scores = None
    keys_to = qs.shape[2]
    halves = (kv[:, :width, :].reshape(tokens, wkv), kv_x[...].reshape(tokens, wkv))
    for p in range(2):
        query = qs[p]
        zero = jnp.zeros_like(query)
        stack = jnp.concatenate(
            [jnp.where(lane < piece, query, zero), jnp.where(lane >= piece, query, zero)], 0
        )
        term = lax.dot_general(
            stack, halves[p][:, :keys_to], (((1,), (1,)), ((), ())),
            preferred_element_type=jnp.float32,
        )
        scores = term if scores is None else scores + term
    scores = scores * ((2 * piece) ** (-0.5)) + bias
    top = jnp.maximum(jnp.max(scores, axis=1, keepdims=True), 0.0)
    raised = jnp.exp(scores - top)
    denominator = jnp.sum(raised, axis=1, keepdims=True) + zero_tokens * jnp.exp(-top)
    weights = raised.astype(jnp.bfloat16)
    attended = []
    for p in range(2):
        value = halves[p][:, wkv - ow.shape[1] :]
        mixed = jnp.dot(weights, value, preferred_element_type=jnp.float32) / denominator
        at = lax.broadcasted_iota(jnp.int32, (rows, ow.shape[1]), 1)
        both = jnp.where(at < gap + piece, mixed[:rows], mixed[rows:])
        attended.append(jnp.where(at < gap, 0.0, both).astype(jnp.bfloat16))
    for copy in ow_copies:
        copy.wait()
    half = out_ref.shape[2]

    def share(side):
        where = pl.ds(pl.multiple_of(side * half, 128), half)
        return jnp.dot(
            attended[0], ow[0, :, where], preferred_element_type=jnp.float32
        ) + jnp.dot(attended[1], ow[1, :, where], preferred_element_type=jnp.float32)

    part_x[...] = share(1 - h).astype(jnp.bfloat16)
    swap = remote(part_x, part_in, p_sem.at[0], p_sem.at[1], core_peer)
    swap.start()
    kept = share(h)
    swap.wait_recv()
    out_ref[0] = (kept + part_in[...].astype(jnp.float32)).astype(jnp.bfloat16)

    swap.wait_send()
    for copy in (core_a, x_a, both_a, core_b, x_b, both_b, *moves_t[0], *moves_t[1], q_to_x):
        copy.wait_send()
    for d in range(shards):
        for w in range(parts):
            x_copy(d, w).wait_send()

    @pl.when(has_hi)
    def _():
        to_hi.wait_send()

    @pl.when(has_lo)
    def _():
        to_lo.wait_send()

    for d in range(shards - 1):
        for w in range(parts):
            @pl.when((s - d >= 0) & has_hi)
            def _(w=w, d=d):
                z_copy(0, w, s - d, d).wait_send()

            @pl.when((s + d < shards) & has_lo)
            def _(w=w, d=d):
                z_copy(1, w, s + d, d).wait_send()


def fused(shards, dna, offsets, stem_weight, conv_weight, qkv_weight, out_weight):
    rows, features = dna.shape
    cols = stem_weight.shape[1]
    taps = conv_weight.shape[0]
    depth = qkv_weight.shape[0]
    masks = offsets.shape[0]
    piece = qkv_weight.shape[3]
    width = out_weight.shape[1]
    wkv = 4 * piece
    query_pad = -(2 * piece) % 128
    qkv = jnp.transpose(qkv_weight, (1, 2, 3, 0)).reshape(6 * piece, depth)
    wq = 2 * piece + query_pad
    deep = wkv - (2 * piece // 128) * 128
    stack = rows + 2 * HALO
    trows = rows + masks * TILE
    bf, f32 = jnp.bfloat16, jnp.float32
    dma = pltpu.SemaphoreType.DMA
    anywhere = pl.BlockSpec(memory_space=pltpu.HBM)
    return pl.pallas_call(
        fused_kernel,
        out_shape=pltpu.VMEM((1, rows, width // 2), bf),
        in_specs=[
            anywhere, anywhere, anywhere, anywhere, anywhere, anywhere,
        ],
        out_specs=pl.BlockSpec(memory_space=pltpu.VMEM),
        scratch_shapes=[
            pltpu.SMEM((masks,), jnp.int32),
            pltpu.VMEM((rows, features), bf),
            pltpu.VMEM((TILE, features), bf),
            pltpu.VMEM((TILE, features), bf),
            pltpu.VMEM((features, cols), bf),
            pltpu.VMEM((4, taps, cols, cols), bf),
            pltpu.VMEM((4, wkv + wq, cols), bf),
            pltpu.VMEM((2, deep, width), bf),
            pltpu.VMEM((4, rows + TILE, cols), bf),
            pltpu.VMEM((stack, cols), f32),
            pltpu.VMEM((taps, stack, cols), f32),
            pltpu.VMEM((4, trows, cols), bf),
            pltpu.VMEM((shards, trows, wkv), bf),
            pltpu.VMEM((shards, rows + TILE, wkv), bf),
            pltpu.VMEM((trows, wq), bf),
            pltpu.VMEM((2, rows, wq), bf),
            pltpu.VMEM((rows, wq), bf),
            pltpu.VMEM((rows, width // 2), bf),
            pltpu.VMEM((rows, width // 2), bf),
            dma((23,)),
            dma((2,)),
            dma((2,)),
            dma((12,)),
            dma((12,)),
            dma((4 * shards + 1,)),
            dma((4 * shards + 1,)),
            dma((8 * shards,)),
            dma((8 * shards,)),
            dma((2,)),
        ],
        compiler_params=pltpu.CompilerParams(
            collective_id=0, has_side_effects=True, vmem_limit_bytes=62 * 2**20
        ),
    )(offsets, dna, stem_weight, conv_weight, qkv, out_weight)


def solution(mesh):
    placed = (
        P(("grp", "seq"), None),
        P("grp"),
        P(None, ("mask", "head")),
        P(None, None, ("mask", "head")),
        P(None, None, "head", "mask"),
        P("head", None),
    )
    shape = mesh.shape

    def body(*arrays):
        piece, cols = arrays[4].shape[3], arrays[2].shape[1]
        fits = piece % 32 == 0 and cols % 128 == 0 and arrays[0].shape[0] >= EARLY + 2 * TILE
        if shape["mask"] == 2 and shape["head"] == 2 and arrays[1].shape[0] == 2 and fits:
            return fused(shape["seq"], *arrays)
        return local(*arrays)

    return jax.shard_map(
        body,
        mesh=mesh,
        in_specs=placed,
        out_specs=P(("grp", "mask"), "seq", "head"),
        check_vma=False,
    )
```

```python
import jax
import jax.numpy as jnp
from jax import lax
from jax.experimental import pallas as pl
from jax.experimental.pallas import tpu as pltpu
from jax.sharding import PartitionSpec as P

BPT = 128
MASK_DEV = 1
WIN_BP = 2048
WROWS = 24


def padded(cells, sides, width):
    for axis, dim in sides:
        count = lax.axis_size(axis)
        ends = count - 1
        head = lax.slice_in_dim(cells, 0, width, axis=dim)
        tail = lax.slice_in_dim(cells, cells.shape[dim] - width, cells.shape[dim], axis=dim)
        cells = jnp.concatenate(
            [
                lax.ppermute(tail, axis, [(i, (i + 1) % count) for i in range(ends)]),
                cells,
                lax.ppermute(head, axis, [((i + 1) % count, i) for i in range(ends)]),
            ],
            axis=dim,
        )
    return cells


def conv_rows(source, weight, out_rows):
    summed = None
    for kernel_tap in range(weight.shape[0]):
        tap_rows = lax.slice_in_dim(source, kernel_tap, kernel_tap + out_rows, axis=source.ndim - 2)
        tap_term = jnp.einsum(
            "...rc,cd->...rd", tap_rows, weight[kernel_tap], preferred_element_type=jnp.float32
        )
        summed = tap_term if summed is None else summed + tap_term
    return summed


def local(dna, offsets, stem_weight, conv_weight, qkv_weight, out_weight):
    tok_rows, features = dna.shape
    margin = conv_weight.shape[0] // 2
    row_start = lax.axis_index("seq") * tok_rows
    masks_all = offsets.shape[0]
    window_rows = WROWS
    span_rows = window_rows + 2 * margin
    extended = padded(dna, (("seq", 0),), margin)
    first_token = offsets // BPT
    local_start = jnp.clip(first_token - margin - row_start, 0, tok_rows - window_rows)

    def cut_window(window_begin):
        return lax.dynamic_slice_in_dim(extended, window_begin, span_rows, 0)

    window_dna = jax.vmap(cut_window)(local_start)
    row_steps = lax.iota(jnp.int32, span_rows)
    base_pair = lax.iota(jnp.int32, features) // 4
    positions = (
        row_start + local_start[:, None, None] - margin + row_steps[None, :, None]
    ) * BPT + base_pair[None, None, :]
    inside = (positions >= offsets[:, None, None]) & (positions < offsets[:, None, None] + WIN_BP)
    masked = jnp.where(inside, jnp.zeros_like(window_dna), window_dna)
    stacked = jnp.concatenate([extended, masked.reshape(masks_all * span_rows, features)], 0)
    embedded = jnp.dot(stacked, stem_weight, preferred_element_type=jnp.float32).astype(
        jnp.bfloat16
    )
    columns = embedded.shape[1]
    base_length = tok_rows + 2 * margin
    shard_part = lax.all_gather(embedded, ("mask", "head"), axis=1, tiled=True)
    part_width = shard_part.shape[1]
    base_out = conv_rows(shard_part[:base_length], conv_weight, tok_rows)
    window_part = shard_part[base_length:].reshape(masks_all, span_rows, part_width)
    window_out = conv_rows(window_part, conv_weight, window_rows)
    convolved = jnp.concatenate([base_out, window_out.reshape(masks_all * window_rows, columns)], 0)
    window_emb = embedded[base_length:].reshape(masks_all, span_rows, columns)[
        :, margin : margin + window_rows
    ]
    own_embedded = jnp.concatenate(
        [
            embedded[margin : margin + tok_rows],
            window_emb.reshape(masks_all * window_rows, columns),
        ],
        0,
    )
    trunk_part = (own_embedded.astype(jnp.float32) + jax.nn.gelu(convolved)).astype(jnp.bfloat16)
    trunk = lax.all_gather(trunk_part, ("mask", "head"), axis=1, tiled=True)
    width_all = trunk.shape[1]
    first_own = lax.axis_index("mask") * MASK_DEV
    own_windows = lax.dynamic_slice_in_dim(
        trunk[tok_rows:].reshape(masks_all, window_rows, width_all), first_own, MASK_DEV, 0
    )
    trunk_rows = jnp.concatenate(
        [trunk[:tok_rows], own_windows.reshape(MASK_DEV * window_rows, width_all)], 0
    )
    wide = trunk_rows.astype(jnp.float32)
    normed = (wide * lax.rsqrt(jnp.mean(wide * wide, axis=1, keepdims=True) + 1e-06)).astype(
        jnp.bfloat16
    )
    projected = jnp.einsum(
        "rd,dthc->rthc",
        normed,
        lax.all_gather(qkv_weight, "mask", axis=3, tiled=True),
        preferred_element_type=jnp.float32,
    ).astype(jnp.bfloat16)
    heads_here = projected.shape[2]
    head_size = projected.shape[3]
    base_qkv = projected[:tok_rows]
    window_qkv = projected[tok_rows:].reshape(MASK_DEV, window_rows, 3, heads_here, head_size)
    own_start = lax.dynamic_slice_in_dim(local_start, first_own, MASK_DEV, 0)
    scaling = head_size ** (-0.5)
    merged = lax.dynamic_update_slice_in_dim(base_qkv, window_qkv[0], own_start[0], 0)
    queries = merged[:, 0]
    running_top = jnp.full((heads_here, tok_rows), -1e30, jnp.float32)
    key_part = lax.all_gather(merged[:, 1], "seq", axis=0, tiled=True)
    value_part = lax.all_gather(merged[:, 2], "seq", axis=0, tiled=True)
    scores = (
        jnp.einsum("qhc,khc->hqk", queries, key_part, preferred_element_type=jnp.float32) * scaling
    )
    new_top = jnp.maximum(running_top, jnp.max(scores, axis=2))
    raised = jnp.exp(scores - new_top[:, :, None])
    denominator = jnp.sum(raised, axis=2)
    weighted = jnp.einsum(
        "hqk,khc->hqc", raised.astype(jnp.bfloat16), value_part, preferred_element_type=jnp.float32
    )
    running_top, denominator, weighted = (new_top, denominator, weighted)
    results = [weighted / denominator[:, :, None]]
    attended = jnp.stack(results).astype(jnp.bfloat16)
    attended = jnp.transpose(attended, (0, 2, 1, 3)).reshape(
        MASK_DEV, tok_rows, heads_here * head_size
    )
    partial_sums = jnp.einsum(
        "mqc,cd->mqd", attended, out_weight, preferred_element_type=jnp.float32
    )
    mixed = lax.psum_scatter(
        partial_sums.astype(jnp.bfloat16), "head", scatter_dimension=2, tiled=True
    )
    return mixed


MESH = pl.DeviceIdType.MESH
HALO = 8
TILE = 16
EARLY = 96
GROUP = 8


def fused_kernel(
    offsets_hbm, dna_hbm, stem_hbm, conv_hbm, qkv_hbm, ow_hbm, out_ref,
    offsets_ref, dna_ref, edge_out, edge_in, stem, cw, qw, ow, emb, emb_own, acc, trunk, kv, kv_x, qa, qs, q_x,
    part_x, part_in,
    w_sem, edge_send, edge_recv, ag_send, ag_recv, x_send, x_recv, z_send, z_recv, p_sem,
):
    rows, features = dna_ref.shape
    cols = stem.shape[1]
    piece = ow_hbm.shape[0] // 4
    wkv, nq = 4 * piece, 2 * piece
    shards = kv.shape[0]
    taps = cw.shape[1]
    margin = taps // 2
    spread = WIN_BP // BPT
    masks = offsets_ref.shape[0]
    m, h, s = lax.axis_index("mask"), lax.axis_index("head"), lax.axis_index("seq")
    row_start = s * rows
    core_peer = {"head": 1 - h}
    x_peer = {"mask": 1 - m}
    cross_peer = {"mask": 1 - m, "head": 1 - h}
    has_lo, has_hi = s > 0, s < shards - 1

    def remote(src, dst, send, recv, device):
        return pltpu.make_async_remote_copy(
            src_ref=src, dst_ref=dst, send_sem=send, recv_sem=recv,
            device_id=device, device_id_type=MESH,
        )

    barrier = pltpu.get_barrier_semaphore()
    for peer in (core_peer, x_peer, cross_peer):
        pl.semaphore_signal(barrier, inc=1, device_id=peer, device_id_type=MESH)

    @pl.when(has_lo)
    def _():
        pl.semaphore_signal(barrier, inc=1, device_id={"seq": s - 1}, device_id_type=MESH)

    @pl.when(has_hi)
    def _():
        pl.semaphore_signal(barrier, inc=1, device_id={"seq": s + 1}, device_id_type=MESH)

    slot_of = (2 * m + h, 2 * m + 1 - h, 2 * (1 - m) + 1 - h, 2 * (1 - m) + h)
    stem_copy = pltpu.make_async_copy(stem_hbm, stem, w_sem.at[0])
    dna_copy = pltpu.make_async_copy(dna_hbm, dna_ref, w_sem.at[21])
    dna_copy.start()
    off_copy = pltpu.make_async_copy(offsets_hbm, offsets_ref, w_sem.at[22])
    off_copy.start()
    stem_copy.start()
    conv_copies, qkv_copies, ow_copies = [], [], []
    for r in range(4):
        span = pl.ds(pl.multiple_of(slot_of[r] * cols, 128), cols)
        conv_copies.append(
            pltpu.make_async_copy(conv_hbm.at[:, span, :], cw.at[r], w_sem.at[1 + r])
        )
        conv_copies[r].start()
    for r in range(4):
        span = pl.ds(pl.multiple_of(slot_of[r] * cols, 128), cols)
        for k, (src, dst, count) in enumerate(((nq, 0, wkv), (0, wkv, nq))):
            copy = pltpu.make_async_copy(
                qkv_hbm.at[pl.ds(src, count), span],
                qw.at[r, pl.ds(dst, count), :],
                w_sem.at[13 + 2 * r + k],
            )
            copy.start()
            qkv_copies.append(copy)
    qw[:, wkv + nq :, :] = jnp.zeros((4, qw.shape[1] - wkv - nq, cols), qw.dtype)
    gap = ow.shape[1] - 2 * piece
    ow[:, 0:gap, :] = jnp.zeros((2, gap, ow.shape[2]), ow.dtype)
    for p, place in enumerate((m, 1 - m)):
        for hh in range(2):
            first = pl.multiple_of(hh * 2 * piece + place * piece, 16)
            copy = pltpu.make_async_copy(
                ow_hbm.at[pl.ds(first, piece), :],
                ow.at[p, pl.ds(gap + hh * piece, piece), :],
                w_sem.at[9 + 2 * p + hh],
            )
            copy.start()
            ow_copies.append(copy)
    past = HALO + rows + HALO
    dna_copy.wait()
    stem_copy.wait()
    emb_inner = jnp.dot(
        dna_ref[...], stem[...], preferred_element_type=jnp.float32
    ).astype(jnp.bfloat16)
    emb[0, :rows] = emb_inner
    emb_own[HALO : HALO + rows] = emb_inner.astype(jnp.float32)

    def first_of(offset):
        return lax.shift_right_logical(offset, 7) - row_start

    off_copy.wait()
    edge = HALO + 2
    row = lax.broadcasted_iota(jnp.int32, (3 * TILE, 1), 0)
    tile = (row >= TILE).astype(jnp.int32) + (row >= 2 * TILE).astype(jnp.int32)
    row = row - tile * TILE
    column = lax.shift_right_logical(lax.broadcasted_iota(jnp.int32, (3 * TILE, features), 1), 2)
    upper = (tile == 0) & (row >= HALO - margin) & (row < HALO)
    source = jnp.where(upper, rows + row - HALO, -1)
    lower = (tile == 1) & (row >= HALO) & (row < HALO + margin)
    source = jnp.where(lower, row - HALO, source)
    cleared = jnp.zeros((3 * TILE, features), jnp.bool_)
    for k in range(masks):
        offset = offsets_ref[k]
        first = first_of(offset)
        phase = offset & (BPT - 1)
        for side in range(2):
            here = row == edge + 2 * k + side
            source = jnp.where(here, first + side * spread, source)
            hidden = column >= phase if side == 0 else column < phase
            cleared = cleared | (here & hidden)
    take = lax.broadcasted_iota(jnp.int32, (3 * TILE, rows), 1) == source
    outer = jnp.dot(
        take.astype(jnp.float32).astype(jnp.bfloat16), dna_ref[...],
        preferred_element_type=jnp.float32,
    )
    outer = jnp.where(cleared, 0.0, outer).astype(jnp.bfloat16)
    emb_edge = jnp.dot(outer, stem[...], preferred_element_type=jnp.float32).astype(jnp.bfloat16)
    for t in range(3):
        edge_out[t] = emb_edge[t * TILE : (t + 1) * TILE]

    steps = has_lo.astype(jnp.int32) + has_hi.astype(jnp.int32)
    pl.semaphore_wait(barrier, 3 + steps)

    def edge_copy(t, n, device):
        return remote(edge_out.at[t], edge_in.at[n], edge_send.at[n], edge_recv.at[n], device)

    up = edge_copy(0, 0, {"seq": s + 1})
    down = edge_copy(1, 1, {"seq": s - 1})

    def gather(buf, g, cuts):
        def pair(src, dst, where, k, device):
            n = 3 * (2 * g + where) + k
            span = pl.ds(cuts[where], cuts[where + 1] - cuts[where])
            return remote(
                buf.at[src, span, :], buf.at[dst, span, :], ag_send.at[n], ag_recv.at[n], device
            )

        return [
            (pair(0, 1, w, 0, core_peer), pair(0, 2, w, 1, cross_peer), pair(2, 3, w, 2, core_peer))
            for w in range(2)
        ]

    (core_a, x_a, both_a), (core_b, x_b, both_b) = gather(emb, 0, (0, rows, rows + TILE))
    @pl.when(has_hi)
    def _():
        up.start()

    @pl.when(has_lo)
    def _():
        down.start()

    x_a.start()
    core_a.start()

    @pl.when(jnp.logical_not(has_lo))
    def _():
        edge_in[0] = jnp.zeros(edge_in.shape[1:], edge_in.dtype)

    @pl.when(jnp.logical_not(has_hi))
    def _():
        edge_in[1] = jnp.zeros(edge_in.shape[1:], edge_in.dtype)

    def conv(r, begin, end):
        for j in range(taps):
            term = jnp.dot(emb[r, begin:end], cw[r, j], preferred_element_type=jnp.float32)
            inner = min(end, rows) - begin
            if inner > 0:
                where = slice(HALO + begin, HALO + begin + inner)
                acc[j, where] = term[:inner] if r == 0 else acc[j, where] + term[:inner]
            if end > rows:
                low, high = term[inner : inner + HALO], term[inner + HALO :]
                acc[j, :HALO] = low if r == 0 else acc[j, :HALO] + low
                where = slice(HALO + rows, past)
                acc[j, where] = high if r == 0 else acc[j, where] + high

    conv_copies[0].wait()
    conv(0, 0, rows)

    @pl.when(has_lo)
    def _():
        up.wait_recv()

    @pl.when(has_hi)
    def _():
        down.wait_recv()

    lower = edge_in[0].astype(jnp.float32) + edge_in[1].astype(jnp.float32)
    emb_wide = edge_out[2].astype(jnp.float32) + lower
    emb[0, rows:] = emb_wide.astype(jnp.bfloat16)
    x_b.start()
    core_b.start()
    emb_own[:HALO] = emb_wide[:HALO]
    emb_own[HALO + rows : past] = emb_wide[HALO:]
    conv(0, rows, rows + TILE)
    core_a.wait_recv()
    core_b.wait_recv()
    conv_copies[1].wait()
    conv(1, 0, rows + TILE)
    x_a.wait_recv()
    both_a.start()
    conv_copies[2].wait()
    conv(2, 0, rows)
    both_a.wait_recv()
    conv_copies[3].wait()
    conv(3, 0, rows)

    def trunk_rows(begin, count):
        begin = begin + HALO
        convolved = acc[0, pl.ds(begin - margin, count), :]
        for j in range(1, taps):
            convolved = convolved + acc[j, pl.ds(begin - margin + j, count), :]
        return emb_own[pl.ds(begin, count), :] + jax.nn.gelu(convolved)

    def window_rows(k, side):
        token = jnp.clip(
            first_of(offsets_ref[k]) + side * spread, -margin, rows + margin - 1
        ) + HALO
        own = HALO + rows + 2 + 2 * k + side
        step = lax.broadcasted_iota(jnp.int32, (GROUP, cols), 0)
        convolved = jnp.zeros((GROUP, cols), jnp.float32)
        center = jnp.where(step == margin, emb_own[own : own + 1, :], 0.0)
        for i in range(taps):
            total = acc[taps - 1 - i, own : own + 1, :]
            for j in range(taps):
                away = i + j - 2 * margin
                if away < 0 if side == 0 else away > 0:
                    total = total + acc[j, pl.ds(token + away, 1), :]
            convolved = jnp.where(step == i, total, convolved)
            away = i - margin
            if away < 0 if side == 0 else away > 0:
                center = jnp.where(step == i, emb_own[pl.ds(token + away, 1), :], center)
        return center + jax.nn.gelu(convolved)

    trunk[0, :EARLY] = trunk_rows(TILE, EARLY).astype(jnp.bfloat16)
    moves_t = gather(trunk, 1, (0, EARLY, trunk.shape[1]))
    moves_t[0][1].start()
    moves_t[0][0].start()
    x_b.wait_recv()
    both_b.start()
    conv(2, rows, rows + TILE)
    both_b.wait_recv()
    conv(3, rows, rows + TILE)
    late = [trunk_rows(0, TILE), trunk_rows(TILE + EARLY, rows - TILE - EARLY)]
    for k in range(masks):
        late += [window_rows(k, 0), window_rows(k, 1)]
    trunk[0, EARLY:] = jnp.concatenate(late, 0).astype(jnp.bfloat16)
    moves_t[1][1].start()
    moves_t[1][0].start()

    for copy in qkv_copies:
        copy.wait()

    def project(w, begin, end):
        by_core, by_x, by_both = moves_t[w]
        total = projected = None
        for r in range(4):
            if r == 1:
                by_core.wait_recv()
            if r == 2:
                by_x.wait_recv()
                by_both.start()
            if r == 3:
                by_both.wait_recv()
            block = trunk[r, begin:end]
            wide = block.astype(jnp.float32)
            square = jnp.sum(wide * wide, axis=1, keepdims=True)
            term = lax.dot_general(
                block, qw[r], (((1,), (1,)), ((), ())), preferred_element_type=jnp.float32
            )
            total = square if r == 0 else total + square
            projected = term if r == 0 else projected + term
        return (projected * lax.rsqrt(total / (4 * cols) + 1e-06)).astype(jnp.bfloat16)

    own_end = rows + TILE
    pieces = (
        (0, 48, 0, 48, 0),
        (48, EARLY, 48, EARLY - 48, 48),
        (EARLY, rows, EARLY, rows - EARLY, EARLY),
        (rows, rows + 2 * TILE, own_end, TILE, rows),
    )
    parts = len(pieces)

    def x_copy(shard, w):
        _, _, begin, count, to = pieces[w]
        n = shard * parts + w
        return remote(
            kv.at[shard, pl.ds(begin, count), :], kv_x.at[shard, pl.ds(to, count), :],
            x_send.at[n], x_recv.at[n], x_peer,
        )

    def z_copy(direction, w, shard, d):
        n = (direction * parts + w) * shards + d
        span = pl.ds(pieces[w][0], pieces[w][1] - pieces[w][0])
        return remote(
            kv.at[shard, span, :], kv.at[shard, span, :], z_send.at[n], z_recv.at[n],
            {"seq": s + (1 if direction == 0 else -1)},
        )

    def send_own(w):
        @pl.when(has_hi)
        def _():
            z_copy(0, w, s, 0).start()

        @pl.when(has_lo)
        def _():
            z_copy(1, w, s, 0).start()

        x_copy(s, w).start()

    def pass_on(w, d):
        @pl.when(s - d >= 0)
        def _():
            z_copy(0, w, s - d, d - 1).wait_recv()

        @pl.when((s - d >= 0) & has_hi)
        def _():
            z_copy(0, w, s - d, d).start()

        @pl.when(s - d >= 0)
        def _():
            x_copy(s - d, w).start()

        @pl.when(s + d < shards)
        def _():
            z_copy(1, w, s + d, d - 1).wait_recv()

        @pl.when((s + d < shards) & has_lo)
        def _():
            z_copy(1, w, s + d, d).start()

        @pl.when(s + d < shards)
        def _():
            x_copy(s + d, w).start()

    early = project(0, 0, EARLY)
    kv[s, :EARLY] = early[:, :wkv]
    send_own(0)
    send_own(1)
    qa[:EARLY] = early[:, wkv:]
    late = project(1, EARLY, trunk.shape[1])
    base_late = rows - EARLY
    kv[s, EARLY:rows] = late[:base_late, :wkv]
    send_own(2)
    two = late[base_late:, :wkv].astype(jnp.float32)
    zeroth = m == 0
    kv[s, rows:own_end] = jnp.where(zeroth, two[:TILE], two[TILE:]).astype(jnp.bfloat16)
    kv[s, own_end:] = jnp.where(zeroth, two[TILE:], two[:TILE]).astype(jnp.bfloat16)
    send_own(3)
    qa[EARLY:] = late[:, wkv:]

    def queries(k):
        first = first_of(offsets_ref[k])
        shape = (rows, qa.shape[0])
        token = lax.broadcasted_iota(jnp.int32, shape, 0)
        place = jnp.where(token < TILE, token + EARLY, token)
        place = jnp.where((token >= TILE) & (token < TILE + EARLY), token - TILE, place)
        begin = rows + k * TILE
        for side in range(2):
            step = token - first - side * spread + margin
            place = jnp.where(
                (step >= 0) & (step < taps), begin + side * GROUP + step, place
            )
        step = token - first
        place = jnp.where((step > margin) & (step < spread - margin), -1, place)
        pick = lax.broadcasted_iota(jnp.int32, shape, 1) == place
        return jnp.dot(
            pick.astype(jnp.float32).astype(jnp.bfloat16), qa[...],
            preferred_element_type=jnp.float32,
        ).astype(jnp.bfloat16)

    q_x[...] = queries(1 - m)
    q_to_x = remote(
        q_x, qs.at[1], x_send.at[shards * parts], x_recv.at[shards * parts], x_peer
    )
    q_to_x.start()
    qs[0] = queries(m)

    width = own_end
    tokens = shards * width
    key = lax.broadcasted_iota(jnp.int32, (1, tokens), 1)
    owner = jnp.zeros((1, tokens), jnp.int32)
    for d in range(1, shards):
        owner = owner + (key >= d * width).astype(jnp.int32)
    key = key - owner * width
    first = lax.shift_right_logical(offsets_ref[m], 7)
    local_token = jnp.where(key < EARLY, key + TILE, key)
    local_token = jnp.where((key >= EARLY) & (key < EARLY + TILE), key - EARLY, local_token)
    token = local_token + owner * rows - first
    kept_base = (key < rows) & ((token < -margin) | (token > spread + margin))
    slot = key - rows
    second = slot >= GROUP
    slot = jnp.where(second, slot - GROUP, slot)
    token = first - margin + slot + jnp.where(second, spread, 0) - owner * rows
    kept_window = (key >= rows) & (slot < taps) & (token >= 0) & (token < rows)
    bias = jnp.where(kept_base | kept_window, 0.0, -1e30)
    zero_tokens = spread - 2 * margin - 1

    for d in range(1, shards):
        for w in range(parts):
            pass_on(w, d)
    q_to_x.wait_recv()
    for d in range(shards):
        for w in range(parts):
            x_copy(d, w).wait_recv()

    lane = lax.broadcasted_iota(jnp.int32, (rows, qs.shape[2]), 1)
    scores = None
    keys_to = qs.shape[2]
    halves = (kv[:, :width, :].reshape(tokens, wkv), kv_x[...].reshape(tokens, wkv))
    for p in range(2):
        query = qs[p]
        zero = jnp.zeros_like(query)
        stack = jnp.concatenate(
            [jnp.where(lane < piece, query, zero), jnp.where(lane >= piece, query, zero)], 0
        )
        term = lax.dot_general(
            stack, halves[p][:, :keys_to], (((1,), (1,)), ((), ())),
            preferred_element_type=jnp.float32,
        )
        scores = term if scores is None else scores + term
    scores = scores * ((2 * piece) ** (-0.5)) + bias
    top = jnp.maximum(jnp.max(scores, axis=1, keepdims=True), 0.0)
    raised = jnp.exp(scores - top)
    denominator = jnp.sum(raised, axis=1, keepdims=True) + zero_tokens * jnp.exp(-top)
    weights = raised.astype(jnp.bfloat16)
    attended = []
    for p in range(2):
        value = halves[p][:, wkv - ow.shape[1] :]
        mixed = jnp.dot(weights, value, preferred_element_type=jnp.float32) / denominator
        at = lax.broadcasted_iota(jnp.int32, (rows, ow.shape[1]), 1)
        both = jnp.where(at < gap + piece, mixed[:rows], mixed[rows:])
        attended.append(jnp.where(at < gap, 0.0, both).astype(jnp.bfloat16))
    for copy in ow_copies:
        copy.wait()
    half = out_ref.shape[2]

    def share(side):
        where = pl.ds(pl.multiple_of(side * half, 128), half)
        return jnp.dot(
            attended[0], ow[0, :, where], preferred_element_type=jnp.float32
        ) + jnp.dot(attended[1], ow[1, :, where], preferred_element_type=jnp.float32)

    part_x[...] = share(1 - h).astype(jnp.bfloat16)
    swap = remote(part_x, part_in, p_sem.at[0], p_sem.at[1], core_peer)
    swap.start()
    kept = share(h)
    swap.wait_recv()
    out_ref[0] = (kept + part_in[...].astype(jnp.float32)).astype(jnp.bfloat16)

    swap.wait_send()
    for copy in (core_a, x_a, both_a, core_b, x_b, both_b, *moves_t[0], *moves_t[1], q_to_x):
        copy.wait_send()
    for d in range(shards):
        for w in range(parts):
            x_copy(d, w).wait_send()

    @pl.when(has_hi)
    def _():
        up.wait_send()

    @pl.when(has_lo)
    def _():
        down.wait_send()

    for d in range(shards - 1):
        for w in range(parts):
            @pl.when((s - d >= 0) & has_hi)
            def _(w=w, d=d):
                z_copy(0, w, s - d, d).wait_send()

            @pl.when((s + d < shards) & has_lo)
            def _(w=w, d=d):
                z_copy(1, w, s + d, d).wait_send()


def fused(shards, dna, offsets, stem_weight, conv_weight, qkv_weight, out_weight):
    rows, features = dna.shape
    cols = stem_weight.shape[1]
    taps = conv_weight.shape[0]
    depth = qkv_weight.shape[0]
    masks = offsets.shape[0]
    piece = qkv_weight.shape[3]
    width = out_weight.shape[1]
    wkv = 4 * piece
    query_pad = -(2 * piece) % 128
    qkv = jnp.transpose(qkv_weight, (1, 2, 3, 0)).reshape(6 * piece, depth)
    wq = 2 * piece + query_pad
    deep = wkv - (2 * piece // 128) * 128
    stack = rows + 2 * HALO
    trows = rows + masks * TILE
    bf, f32 = jnp.bfloat16, jnp.float32
    dma = pltpu.SemaphoreType.DMA
    anywhere = pl.BlockSpec(memory_space=pltpu.HBM)
    return pl.pallas_call(
        fused_kernel,
        out_shape=pltpu.VMEM((1, rows, width // 2), bf),
        in_specs=[
            anywhere, anywhere, anywhere, anywhere, anywhere, anywhere,
        ],
        out_specs=pl.BlockSpec(memory_space=pltpu.VMEM),
        scratch_shapes=[
            pltpu.SMEM((masks,), jnp.int32),
            pltpu.VMEM((rows, features), bf),
            pltpu.VMEM((3, TILE, cols), bf),
            pltpu.VMEM((2, TILE, cols), bf),
            pltpu.VMEM((features, cols), bf),
            pltpu.VMEM((4, taps, cols, cols), bf),
            pltpu.VMEM((4, wkv + wq, cols), bf),
            pltpu.VMEM((2, deep, width), bf),
            pltpu.VMEM((4, rows + TILE, cols), bf),
            pltpu.VMEM((stack, cols), f32),
            pltpu.VMEM((taps, stack, cols), f32),
            pltpu.VMEM((4, trows, cols), bf),
            pltpu.VMEM((shards, trows, wkv), bf),
            pltpu.VMEM((shards, rows + TILE, wkv), bf),
            pltpu.VMEM((trows, wq), bf),
            pltpu.VMEM((2, rows, wq), bf),
            pltpu.VMEM((rows, wq), bf),
            pltpu.VMEM((rows, width // 2), bf),
            pltpu.VMEM((rows, width // 2), bf),
            dma((23,)),
            dma((2,)),
            dma((2,)),
            dma((12,)),
            dma((12,)),
            dma((4 * shards + 1,)),
            dma((4 * shards + 1,)),
            dma((8 * shards,)),
            dma((8 * shards,)),
            dma((2,)),
        ],
        compiler_params=pltpu.CompilerParams(
            collective_id=0, has_side_effects=True, vmem_limit_bytes=62 * 2**20
        ),
    )(offsets, dna, stem_weight, conv_weight, qkv, out_weight)


def solution(mesh):
    placed = (
        P(("grp", "seq"), None),
        P("grp"),
        P(None, ("mask", "head")),
        P(None, None, ("mask", "head")),
        P(None, None, "head", "mask"),
        P("head", None),
    )
    shape = mesh.shape

    def body(*arrays):
        piece, cols = arrays[4].shape[3], arrays[2].shape[1]
        fits = piece % 32 == 0 and cols % 128 == 0 and arrays[0].shape[0] >= EARLY + 2 * TILE
        if shape["mask"] == 2 and shape["head"] == 2 and arrays[1].shape[0] == 2 and fits:
            return fused(shape["seq"], *arrays)
        return local(*arrays)

    return jax.shard_map(
        body,
        mesh=mesh,
        in_specs=placed,
        out_specs=P(("grp", "mask"), "seq", "head"),
        check_vma=False,
    )
```
